512 devices in a mesh: frames: 8 (over y), bricks: 64 (over z, x, core).
Axes of the slice: x: 4, y: 8, z: 8, core: 2. Of those that a mesh axis runs over, the one named last changes fastest.
Arguments:
- recording: bfloat16 [128, 256, 16, 256], P('frames', 'bricks'), may hold values from -1 to 2
- traces: bfloat16 [128, 2048], P('frames', 'bricks'), may hold values from 0 to 2
- footprints: bfloat16 [2048, 16384], P('bricks'), may hold values from 0 to 1, as said below
- block_owner: int32 [2048, 1], P('bricks'), may hold values from 0 to 63; in each aligned block of 32 rows (0 to 31, 32 to 63, ...) at most 4 rows name the same one
- block_slot: int32 [2048], P('bricks'), may hold values from 0 to 31
Outputs:
- traces_new: float32 [128, 2048], P('frames', 'bricks')
- footprints_new: bfloat16 [2048, 16384], P('bricks')
The draws below stay inside these ranges and needn't reach their ends.
Inputs may be any that keep to these rules, and one draw needn't show every extreme that they name: `footprints`: each row is positive on exactly 128 voxels forming a run in the slab's flat voxel order taken circularly, and 0 elsewhere; positive entries are at least 0.02. `block_owner`: among the 32 blocks of one slab, at most 4 have the same owner.
All inputs are finite; a program needn't handle non-finite values.
Results may differ from the reference program's by a relative error of at most 0.0033.
Values may be sent and summed in bfloat16 or wider, within the bound.
No kernel may reach another device: no remote copies, remote signals or barrier semaphores. Data moves between devices by JAX's collectives and lax.ppermute only.
A program may use at most 64 MiB of HBM per device.

```python
import math
import jax
import jax.numpy as jnp
import numpy as np
from jax import lax

NZ = 16
NY = 256
K_LOC = 32
FOOT_W = 128
COMP_DEV = 32
SEND_CAP = 4
NF = 128
NX = 256
V_DEV = 16384
NCOMP = 2048
BLOCKS = 2048
OWNERS = 64
N_BRICKS = 64


def draw_footprints(key, part):
    key_center, key_value = jax.random.split(jax.random.fold_in(key, 17))
    centers = jax.random.randint(key_center, (BLOCKS, 1), 0, V_DEV)
    offsets = (jnp.arange(V_DEV, dtype=jnp.int32)[None, :] - centers) % V_DEV
    inside = offsets < FOOT_W
    values = jnp.exp(jax.random.uniform(key_value, (BLOCKS, V_DEV), jnp.float32, math.log(0.02), 0.0))
    return jnp.where(inside, values, 0.0).astype(jnp.bfloat16)


def place_ends(drawn, stream_key, smallest, largest):
    longest = drawn.shape.index(max(drawn.shape))
    spots = []
    for shift in (0, 1):
        where = [jax.random.randint(jax.random.fold_in(stream_key, axis), (), 0, length) for axis, length in enumerate(drawn.shape)]
        where[longest] = (where[longest] + shift) % drawn.shape[longest]
        spots.append(tuple(where))
    return drawn.at[spots[0]].set(smallest).at[spots[1]].set(largest)


def steps_of(key, extent, pieces, low, largest):
    def one(position, blocks):
        steps = jax.random.uniform(jax.random.fold_in(jax.random.fold_in(key, 6), position), (blocks,), jnp.float32, low / len(pieces), largest / len(pieces))
        return jnp.repeat(jnp.exp(steps), extent[position] // blocks).reshape((-1,) + (1,) * (len(extent) - position - 1))

    level = one(*pieces[0])
    for cut in pieces[1:]:
        level = level * one(*cut)
    return level


def shared_out(rng, own, number, rows, amount, top, bound, lean):
    ranking = jax.random.permutation(rng, amount)
    heavy_load, ordinary = portions_of(amount, rows * top, bound, lean, True), portions_of(amount, rows * top, bound, lean, False)
    places = jnp.arange(amount)

    def named(sizes, offset_by):
        used = int((sizes > 0).sum())
        fixed = max(1, used // 4)
        passed = fixed + (places - fixed + offset_by * (used - fixed)) % max(1, amount - fixed)
        return jnp.zeros((amount,), jnp.int32).at[ranking[jnp.where(places < fixed, places, passed)]].set(jnp.asarray(sizes, jnp.int32))

    sizes = jnp.where(number % 4 == 0, named(heavy_load, number // 4), named(ordinary, number - number // 4 - 1))
    mixed = jax.random.permutation(jax.random.fold_in(own, 3), amount)
    source_of, sink = mixed[0:amount // 2 * 2:2], mixed[1:amount // 2 * 2:2]
    margin = jnp.minimum(sizes[source_of] - 1, bound - sizes[sink]) // 2
    margin = jnp.where((source_of == ranking[0]) | (sink == ranking[0]) | (sizes[sink] == 0), 0, jnp.maximum(margin, 0))
    passed = jax.random.randint(jax.random.fold_in(own, 4), (amount // 2,), 0, 1 << 20) % (margin + 1)
    sizes = sizes.at[source_of].add(-passed).at[sink].add(passed)
    labels = jnp.searchsorted(jnp.cumsum(sizes), jnp.arange(rows * top), side="right").astype(jnp.int32)
    table = labels.reshape(top, rows).T
    table = table[jax.random.permutation(jax.random.fold_in(own, 1), rows)]
    offset_by = jax.random.randint(jax.random.fold_in(own, 2), (rows, 1), 0, top)
    return jnp.take_along_axis(table, (jnp.arange(top)[None, :] + offset_by) % top, axis=1)


def portions_of(count, total, most, skew, full):
    weights = [(1 << 20) // math.isqrt(rank ** skew) + 1 for rank in range(1, count + 1)]
    largest = most if full else min(most, max(-(-total // count), total * weights[0] // sum(weights)))
    least = 1 if total - largest >= count - 1 else 0
    given, spare = [largest] + [least] * (count - 1), total - largest - least * (count - 1)
    while spare > 0:
        free = [i for i in range(1, count) if given[i] < largest] or [i for i in range(1, count) if given[i] < most]
        whole, left = sum([weights[i] for i in free]), spare
        for i in free:
            more = min(most - given[i], max(1, left * weights[i] // whole), spare)
            given[i] = given[i] + more
            spare = spare - more
    return np.array(given)


def setup_inputs(seed: int = 0) -> dict:
    key_of = jax.random.split(jax.random.key(seed), 6)
    recording = jnp.clip(-1.0 + 3.0 * jax.random.uniform(key_of[0], (NF, NX, NZ, NY), jnp.float32) ** steps_of(key_of[0], (NF, NX, NZ, NY), ((0, 8), (1, 64)), -0.2, 0.2), -1.0, 2.0).astype(jnp.bfloat16)
    traces = jnp.clip(2.0 * jax.random.uniform(key_of[1], (NF, NCOMP), jnp.float32) ** steps_of(key_of[1], (NF, NCOMP), ((0, 8), (1, 64)), -0.2, 0.2), 0.0, 2.0).astype(jnp.bfloat16)
    footprints = draw_footprints(jax.random.fold_in(key_of[5], 71), 0)
    block_owner_keys = jax.random.split(jax.random.fold_in(key_of[3], 1), BLOCKS // K_LOC)
    block_owner_turns = jax.random.permutation(jax.random.fold_in(key_of[3], 3), BLOCKS // K_LOC)
    block_owner = jax.vmap(lambda own, number: shared_out(jax.random.fold_in(key_of[3], 2), own, number, K_LOC, OWNERS, 1, SEND_CAP, 2))(block_owner_keys, block_owner_turns).reshape((BLOCKS, 1))
    block_slot = place_ends(jax.random.randint(key_of[4], (BLOCKS,), 0, COMP_DEV), jax.random.fold_in(key_of[4], 1), 0, COMP_DEV - 1).astype(jnp.int32)
    return dict(recording=recording, traces=traces, footprints=footprints, block_owner=block_owner, block_slot=block_slot)


TIME_STEP = 0.14
EDGE_SCALE = 1.0


def edge_flux(center, other):
    difference = other - center
    return difference / (1.0 + (difference / EDGE_SCALE) ** 2)


def relax_once(extended):
    center = extended[:, 1:-1]
    padded = jnp.pad(center, ((0, 0), (0, 0), (1, 1), (1, 1)))
    summed_flux = edge_flux(center, extended[:, 2:]) + edge_flux(center, extended[:, :-2])
    summed_flux = summed_flux + edge_flux(center, padded[:, :, 2:, 1:-1]) + edge_flux(center, padded[:, :, :-2, 1:-1])
    summed_flux = summed_flux + edge_flux(center, padded[:, :, 1:-1, 2:]) + edge_flux(center, padded[:, :, 1:-1, :-2])
    return center + TIME_STEP * summed_flux


def smooth_frame(frame):
    current = frame[None].astype(jnp.float32)
    for sweep in range(3):
        extended = jnp.pad(current, ((0, 0), (1, 1), (0, 0), (0, 0)))
        current = relax_once(extended)
    return current[0].astype(jnp.bfloat16)


def reference(recording, traces, footprints, block_owner, block_slot):
    denoised = lax.map(smooth_frame, recording)
    slabs = denoised.reshape(NF, N_BRICKS, V_DEV)
    component = (block_owner[:, 0] * COMP_DEV + block_slot).astype(jnp.int32)
    comp_grid = component.reshape(N_BRICKS, K_LOC)
    foot_grid = footprints.reshape(N_BRICKS, K_LOC, V_DEV)
    previous = traces.astype(jnp.float32)

    def brick_partials(brick_index):
        slab_data = lax.dynamic_index_in_dim(slabs, brick_index, 1, keepdims=False)
        foot = foot_grid[brick_index]
        slot_traces = jnp.take(previous, comp_grid[brick_index], axis=1)
        correlation = jnp.dot(foot, foot.T, preferred_element_type=jnp.float32)
        partial_value = jnp.dot(slab_data, foot.T, preferred_element_type=jnp.float32) - jnp.dot(slot_traces, correlation, precision=lax.Precision.HIGHEST)
        return partial_value.T, jnp.diagonal(correlation)

    partial_rows, diag_rows = lax.map(brick_partials, jnp.arange(N_BRICKS, dtype=jnp.int32))
    summed = jax.ops.segment_sum(partial_rows.reshape(BLOCKS, NF), component, NCOMP)
    diag_sum = jax.ops.segment_sum(diag_rows.reshape(BLOCKS), component, NCOMP)
    traces_new = jnp.maximum(0.0, previous + summed.T / (diag_sum + 1.0)[None, :])
    new_bf = traces_new.astype(jnp.bfloat16)

    def brick_update(brick_index):
        slab_data = lax.dynamic_index_in_dim(slabs, brick_index, 1, keepdims=False)
        foot = foot_grid[brick_index].astype(jnp.float32)
        slot_new = jnp.take(new_bf, comp_grid[brick_index], axis=1)
        product = jnp.dot(slot_new.T, slab_data, preferred_element_type=jnp.float32)
        slot_wide = slot_new.astype(jnp.float32)
        gram = jnp.dot(slot_wide.T, slot_wide, precision=lax.Precision.HIGHEST)
        gradient = product - jnp.dot(gram, foot, precision=lax.Precision.HIGHEST)
        denominator = jnp.diagonal(gram) + 1.0
        stepped = jnp.where(foot > 0, jnp.maximum(foot + gradient / denominator[:, None], 0.0), 0.0)
        return stepped.astype(jnp.bfloat16)

    footprints_new = lax.map(brick_update, jnp.arange(N_BRICKS, dtype=jnp.int32)).reshape(BLOCKS, V_DEV)
    return traces_new, footprints_new
```

```python
import jax
import jax.numpy as jnp
from jax import lax
from jax.experimental import pallas as pl
from jax.experimental.pallas import tpu as pltpu
from jax.sharding import PartitionSpec as P

TIME_STEP = 0.14
HIGHEST = lax.Precision.HIGHEST
LANES = 128


def flux_of(difference):
    return difference / (1.0 + difference * difference)


def halo_planes(recording, width):
    count = lax.axis_size("bricks")
    planes = recording.shape[1]
    tail = lax.slice_in_dim(recording, planes - width, planes, axis=1)
    head = lax.slice_in_dim(recording, 0, width, axis=1)
    low = lax.ppermute(tail, "bricks", [(i, i + 1) for i in range(count - 1)])
    high = lax.ppermute(head, "bricks", [(i + 1, i) for i in range(count - 1)])
    return low, high


def run_starts(footprints):
    inside = footprints > 0
    before = jnp.roll(inside, 1, axis=1)
    place = lax.broadcasted_iota(jnp.int32, footprints.shape, 1)
    return jnp.sum(jnp.where(inside & ~before, place, 0), axis=1, dtype=jnp.int32)


def windows_kernel(starts, foot, windows, corr):
    blocks, voxels = foot.shape
    tiles = voxels // LANES
    lane = lax.broadcasted_iota(jnp.int32, (blocks, LANES), 1)
    acc = jnp.zeros((blocks, LANES), jnp.float32)
    for k in range(blocks):
        start = starts[k]
        first = start // LANES
        second = (first + 1) % tiles
        offset = start - first * LANES
        one = foot[:, pl.ds(pl.multiple_of(first * LANES, LANES), LANES)].astype(jnp.float32)
        two = foot[:, pl.ds(pl.multiple_of(second * LANES, LANES), LANES)].astype(jnp.float32)
        window = jnp.where(lane >= offset, one, two)
        windows[k] = window
        column = jnp.sum(window * window[k : k + 1], axis=1, keepdims=True)
        acc = jnp.where(lane == k, column, acc)
    corr[...] = acc


def foot_windows(starts, footprints):
    blocks, voxels = footprints.shape
    vmem = pl.BlockSpec(memory_space=pltpu.VMEM)
    return pl.pallas_call(
        windows_kernel,
        in_specs=[pl.BlockSpec(memory_space=pltpu.SMEM), vmem],
        out_specs=[vmem, vmem],
        out_shape=[
            jax.ShapeDtypeStruct((blocks, blocks, LANES), jnp.float32),
            jax.ShapeDtypeStruct((blocks, LANES), jnp.float32),
        ],
        name="windows",
    )(starts, footprints)


def relax(planes, low_keep, high_keep, masks):
    first_row, last_row, first_col, last_col = masks
    across = [flux_of(planes[i + 1] - planes[i]) for i in range(len(planes) - 1)]
    out = []
    for i in range(1, len(planes) - 1):
        u = planes[i]
        edge = flux_of(-u)
        rows, cols = u.shape
        nxt = jnp.where(last_row, 0.0, pltpu.roll(u, rows - 1, 0))
        down = flux_of(nxt - u)
        up = jnp.where(first_row, -edge, pltpu.roll(down, 1, 0))
        nxt = jnp.where(last_col, 0.0, pltpu.roll(u, cols - 1, 1))
        right = flux_of(nxt - u)
        left = jnp.where(first_col, -edge, pltpu.roll(right, 1, 1))
        total = (across[i] - across[i - 1]) + (down - up) + (right - left)
        out.append(u + TIME_STEP * total)
    return out


def denoise_kernel(starts, keep, rec, low, high, windows, voxel_windows, projected, field):
    frames, planes, rows, cols = rec.shape
    width = low.shape[1]
    halves = cols // LANES
    low_keep = keep[0]
    high_keep = keep[1]
    row = lax.broadcasted_iota(jnp.int32, (rows, cols), 0)
    col = lax.broadcasted_iota(jnp.int32, (rows, cols), 1)
    masks = (row == 0, row == rows - 1, col == 0, col == cols - 1)

    def one_frame(f, carry):
        u = [low[f, i].astype(jnp.float32) for i in range(width)]
        u = u + [rec[f, i].astype(jnp.float32) for i in range(planes)]
        u = u + [high[f, i].astype(jnp.float32) for i in range(width)]
        for sweep in range(width):
            u = relax(u, low_keep, high_keep, masks)
            extra = width - 1 - sweep
            if extra:
                u = (
                    [v * low_keep for v in u[:extra]]
                    + u[extra : extra + planes]
                    + [v * high_keep for v in u[extra + planes :]]
                )
        for i in range(planes):
            rounded = u[i].astype(jnp.bfloat16).astype(jnp.float32)
            for h in range(halves):
                at = pl.multiple_of(f * (planes * rows) + i * rows, rows)
                field[h, pl.ds(at, rows), :] = rounded[:, h * LANES : (h + 1) * LANES]
        return carry

    lax.fori_loop(0, frames, one_frame, 0)
    blocks = windows.shape[0]
    tiles = planes * rows * halves
    lane = lax.broadcasted_iota(jnp.int32, (frames, LANES), 1)
    acc = jnp.zeros((frames, LANES), jnp.float32)
    for k in range(blocks):
        start = starts[k]
        first = start // LANES
        second = (first + 1) % tiles
        offset = start - first * LANES
        one = field[first % halves, pl.ds(first // halves, frames, stride=planes * rows), :]
        two = field[second % halves, pl.ds(second // halves, frames, stride=planes * rows), :]
        window = jnp.where(lane >= offset, one, two)
        voxel_windows[k] = window
        column = jnp.sum(window * windows[k, k : k + 1, :], axis=1, keepdims=True)
        acc = jnp.where(lane == k, column, acc)
    projected[...] = acc


def denoise_windows(starts, keep, recording, low, high, windows):
    frames, planes, rows, cols = recording.shape
    blocks = windows.shape[0]
    vmem = pl.BlockSpec(memory_space=pltpu.VMEM)
    smem = pl.BlockSpec(memory_space=pltpu.SMEM)
    return pl.pallas_call(
        denoise_kernel,
        in_specs=[smem, smem, vmem, vmem, vmem, vmem],
        out_specs=[vmem, vmem],
        out_shape=[
            jax.ShapeDtypeStruct((blocks, frames, LANES), jnp.float32),
            jax.ShapeDtypeStruct((frames, LANES), jnp.float32),
        ],
        scratch_shapes=[pltpu.VMEM((cols // LANES, frames * planes * rows, LANES), jnp.float32)],
        cost_estimate=pl.CostEstimate(flops=10**9, transcendentals=0, bytes_accessed=20 * 10**6),
        name="denoise",
    )(starts, keep, recording, low, high, windows)


def finish_kernel(starts, products, gram, windows, out):
    blocks, voxels = out.shape
    tiles = voxels // LANES
    lane = lax.broadcasted_iota(jnp.int32, (blocks, LANES), 1)
    row = lax.broadcasted_iota(jnp.int32, (blocks, LANES), 0)
    out[...] = jnp.zeros(out.shape, out.dtype)
    product = jnp.sum(products[...], axis=0)
    for k in range(blocks):
        start = starts[k]
        first = start // LANES
        second = (first + 1) % tiles
        offset = start - first * LANES
        spread = jnp.sum(windows[k] * gram[:, k : k + 1], axis=0, keepdims=True)
        current = windows[k, k : k + 1, :]
        gradient = product[k : k + 1, :] - spread
        stepped = jnp.maximum(current + gradient / (gram[k : k + 1, k : k + 1] + 1.0), 0.0)
        stepped = jnp.where(current > 0, stepped, 0.0)
        at = pl.ds(pl.multiple_of(first * LANES, LANES), LANES)
        old = out[:, at].astype(jnp.float32)
        out[:, at] = jnp.where((row == k) & (lane >= offset), stepped, old).astype(out.dtype)
        at = pl.ds(pl.multiple_of(second * LANES, LANES), LANES)
        old = out[:, at].astype(jnp.float32)
        out[:, at] = jnp.where((row == k) & (lane < offset), stepped, old).astype(out.dtype)


def finish(starts, products, gram, windows, voxels):
    blocks = windows.shape[0]
    vmem = pl.BlockSpec(memory_space=pltpu.VMEM)
    return pl.pallas_call(
        finish_kernel,
        in_specs=[pl.BlockSpec(memory_space=pltpu.SMEM), vmem, vmem, vmem],
        out_specs=vmem,
        out_shape=jax.ShapeDtypeStruct((blocks, voxels), jnp.bfloat16),
        name="finish",
    )(starts, products, gram, windows)


def to_all(piece, axis):
    count = lax.axis_size(axis)
    return lax.all_to_all(jnp.broadcast_to(piece[None], (count,) + piece.shape), axis, 0, 0)


def shards(recording, traces, footprints, block_owner, block_slot):
    frames, owned = traces.shape
    blocks, voxels = footprints.shape
    owners = lax.axis_size("bricks")
    position = lax.axis_index("bricks")
    low, high = halo_planes(recording, 3)
    keep = jnp.stack([position > 0, position < owners - 1]).astype(jnp.float32)
    starts = run_starts(footprints)
    windows, corr = foot_windows(starts, footprints)
    corr = corr[:, :blocks]
    diag = jnp.diagonal(corr)
    owner = block_owner[:, 0]
    component = owner * owned + block_slot

    diag_high = diag.astype(jnp.bfloat16)
    diag_low = (diag - diag_high.astype(jnp.float32)).astype(jnp.bfloat16)
    extra = jnp.stack(
        [owner.astype(jnp.bfloat16), block_slot.astype(jnp.bfloat16), diag_high, diag_low]
    )
    piece = jnp.concatenate([traces.reshape(-1), extra.reshape(-1)]).reshape(-1, LANES)
    piece = jnp.pad(piece, ((0, -piece.shape[0] % 8), (0, 0)))
    prior = to_all(piece, "bricks").reshape(owners, -1).astype(jnp.float32)
    cells = frames * owned
    prior_traces = prior[:, :cells].reshape(owners, frames, owned)
    extras = prior[:, cells : cells + 4 * blocks].reshape(owners, 4, blocks)
    all_owner = extras[:, 0].reshape(-1).astype(jnp.int32)
    all_slot = extras[:, 1].reshape(-1).astype(jnp.int32)
    all_comp = all_owner * owned + all_slot
    all_diag = (extras[:, 2] + extras[:, 3]).reshape(-1)

    voxel_windows, projected = denoise_windows(starts, keep, recording, low, high, windows)
    projected = projected[:, :blocks]

    pick_owner = (owner[:, None] == jnp.arange(owners, dtype=jnp.int32)[None, :]).astype(jnp.bfloat16)
    rows = jnp.dot(
        pick_owner,
        prior[:, :cells].astype(jnp.bfloat16),
        preferred_element_type=jnp.float32,
    ).reshape(blocks, frames, owned)
    pick_slot = block_slot[:, None] == jnp.arange(owned, dtype=jnp.int32)[None, :]
    slot_prior = jnp.sum(jnp.where(pick_slot[:, None, :], rows, 0.0), axis=2).T

    partial_value = projected - jnp.dot(slot_prior, corr, precision=HIGHEST)
    gathered = to_all(partial_value.T.reshape(-1, LANES), "bricks").reshape(owners * blocks, frames)

    mine = position * owned + jnp.arange(owned, dtype=jnp.int32)
    target = jnp.concatenate([mine, component])
    match = (target[:, None] == all_comp[None, :]).astype(jnp.float32)
    summed = jnp.dot(match, gathered, precision=HIGHEST)
    diag_sum = jnp.dot(match, all_diag[:, None], precision=HIGHEST)
    before = jnp.concatenate([traces.astype(jnp.float32).T, slot_prior.T])
    after = jnp.maximum(0.0, before + summed / (diag_sum + 1.0)).T
    traces_new = after[:, :owned]
    slot_new = after[:, owned:].astype(jnp.bfloat16).astype(jnp.float32)

    product_part = jnp.sum(voxel_windows * slot_new.T[:, :, None], axis=1)
    sent = jnp.concatenate(
        [product_part, slot_new.reshape(-1, LANES), jnp.zeros((4, LANES), jnp.float32)]
    )
    shared = to_all(sent, "frames")
    groups = shared.shape[0]
    all_slots = shared[:, blocks : blocks + 4].reshape(groups * frames, blocks)
    gram = lax.dot_general(
        all_slots.astype(jnp.bfloat16),
        all_slots.astype(jnp.bfloat16),
        (((0,), (0,)), ((), ())),
        preferred_element_type=jnp.float32,
    )
    footprints_new = finish(starts, shared[:, :blocks], gram, windows, voxels)
    return (traces_new, footprints_new)


def solution(mesh):
    return jax.shard_map(
        shards,
        mesh=mesh,
        in_specs=(
            P("frames", "bricks", None, None),
            P("frames", "bricks"),
            P("bricks", None),
            P("bricks", None),
            P("bricks"),
        ),
        out_specs=(P("frames", "bricks"), P("bricks", None)),
        check_vma=False,
    )
```

```python
import jax
import jax.numpy as jnp
from jax import lax
from jax.experimental import pallas as pl
from jax.experimental.pallas import tpu as pltpu
from jax.sharding import PartitionSpec as P


TIME_STEP = 0.14
HIGHEST = lax.Precision.HIGHEST
LANES = 128
SUBLANES = 8
F32 = jnp.float32
BF16 = jnp.bfloat16
VMEM = pl.BlockSpec(memory_space=pltpu.VMEM)
SMEM = pl.BlockSpec(memory_space=pltpu.SMEM)


def iota(shape, axis):
    return lax.broadcasted_iota(jnp.int32, shape, axis)


def onehot(mask):
    return jnp.where(mask, 1.0, 0.0).astype(BF16)


def split_run(start, tiles):
    first = start >> 7
    return first, (first + 1) & (tiles - 1), start & (LANES - 1)


def lane_tile(index):
    return pl.ds(pl.multiple_of(index * LANES, LANES), LANES)


def two_terms(value):
    high = value.astype(BF16).astype(F32)
    return high, value - high


def prepare_kernel(base, foot, starts, windows, compact, corr, piece):
    blocks, voxels = foot.shape
    tiles = voxels // LANES
    acc = jnp.zeros((blocks, LANES), BF16)
    for t in range(1, tiles):
        cell = foot[:, t * LANES : (t + 1) * LANES]
        acc = acc + jnp.where(cell > 0, jnp.asarray(t, BF16), jnp.asarray(0, BF16))
    tile_of = acc.astype(F32)
    lowest = jnp.min(tile_of, axis=1, keepdims=True)
    highest = jnp.max(tile_of, axis=1, keepdims=True)
    first_tile = jnp.where(highest - lowest > 1.5, highest, lowest)
    behind = jnp.sum(jnp.where(tile_of != first_tile, 1.0, 0.0), axis=1, keepdims=True)
    begin = (first_tile * LANES + behind).astype(jnp.int32)
    lane = iota((blocks, LANES), 1)
    row = iota((blocks, LANES), 0)
    sums = jnp.zeros((blocks, LANES), F32)
    for k in range(blocks):
        start = begin[k, 0]
        starts[k] = start
        first, second, offset = split_run(start, tiles)
        one = foot[:, lane_tile(first)].astype(F32)
        two = foot[:, lane_tile(second)].astype(F32)
        window = jnp.where(lane >= offset, one, two)
        windows[k] = window.astype(BF16)
        own = window[k : k + 1]
        compact[k : k + 1, :] = own
        sums = jnp.where(lane == k, jnp.sum(window * own, axis=1, keepdims=True), sums)
    corr[...] = sums
    diag = jnp.sum(jnp.where(lane == row, sums, 0.0), axis=1, keepdims=True)
    placed = jnp.where(lane == 2 * SUBLANES + row % SUBLANES, diag, 0.0)
    groups = blocks // SUBLANES
    rows = [
        jnp.sum(placed[q * SUBLANES : (q + 1) * SUBLANES], axis=0, keepdims=True)
        for q in range(groups)
    ]
    terms = [two_terms(r) for r in rows]
    part = jnp.concatenate([t[0] for t in terms] + [t[1] for t in terms], axis=0)
    whole = (base[...] + part).astype(BF16)
    piece[...] = jnp.broadcast_to(whole[None], piece.shape)


def prepare(base, footprints, owners):
    blocks, _ = footprints.shape
    return pl.pallas_call(
        prepare_kernel,
        in_specs=[VMEM, VMEM],
        out_specs=[SMEM, VMEM, VMEM, VMEM, VMEM],
        out_shape=[
            jax.ShapeDtypeStruct((blocks,), jnp.int32),
            jax.ShapeDtypeStruct((blocks, blocks, LANES), BF16),
            jax.ShapeDtypeStruct((blocks, LANES), F32),
            jax.ShapeDtypeStruct((blocks, LANES), F32),
            jax.ShapeDtypeStruct((owners, SUBLANES, LANES), BF16),
        ],
        name="prepare",
    )(base, footprints)


def flux_of(difference):
    return difference / (1.0 + difference * difference)


def relax(planes, masks):
    first_row, last_row, first_col, last_col = masks
    across = [
        [[flux_of(planes[i + 1][z][y] - planes[i][z][y]) for y in range(2)] for z in range(2)]
        for i in range(len(planes) - 1)
    ]
    out = []
    for i in range(1, len(planes) - 1):
        u = planes[i]
        edge = [[flux_of(u[0][0]), flux_of(u[0][1])], [flux_of(u[1][0]), None]]
        total = [[across[i][z][y] - across[i - 1][z][y] for y in range(2)] for z in range(2)]
        for y in range(2):
            low = pltpu.roll(u[0][y], SUBLANES - 1, 0)
            high = pltpu.roll(u[1][y], SUBLANES - 1, 0)
            down_low = flux_of(jnp.where(last_row, high, low) - u[0][y])
            down_high = flux_of(jnp.where(last_row, 0.0, high) - u[1][y])
            up_low = pltpu.roll(down_low, 1, 0)
            up_high = pltpu.roll(down_high, 1, 0)
            total[0][y] = total[0][y] + (down_low - jnp.where(first_row, edge[0][y], up_low))
            total[1][y] = total[1][y] + (down_high - jnp.where(first_row, up_low, up_high))
        for z in range(2):
            low = pltpu.roll(u[z][0], LANES - 1, 1)
            high = pltpu.roll(u[z][1], LANES - 1, 1)
            right_low = flux_of(jnp.where(last_col, high, low) - u[z][0])
            right_high = flux_of(jnp.where(last_col, 0.0, high) - u[z][1])
            left_low = pltpu.roll(right_low, 1, 1)
            left_high = pltpu.roll(right_high, 1, 1)
            total[z][0] = total[z][0] + (right_low - jnp.where(first_col, edge[z][0], left_low))
            total[z][1] = total[z][1] + (right_high - jnp.where(first_col, left_low, left_high))
        out.append([[u[z][y] + TIME_STEP * total[z][y] for y in range(2)] for z in range(2)])
    return out


def quarters(plane):
    wide = plane.astype(F32)
    return [
        [wide[z * SUBLANES : (z + 1) * SUBLANES, y * LANES : (y + 1) * LANES] for y in range(2)]
        for z in range(2)
    ]


def scaled(plane, keep):
    return [[cell * keep for cell in line] for line in plane]


def denoise_kernel(starts, rec, low, high, compact, voxel_windows, projected, field):
    frames, planes, rows, _ = rec.shape
    width = low.shape[1]
    position = lax.axis_index("bricks")
    low_keep = jnp.where(position > 0, 1.0, 0.0)
    high_keep = jnp.where(position < lax.axis_size("bricks") - 1, 1.0, 0.0)
    row = iota((SUBLANES, LANES), 0)
    col = iota((SUBLANES, LANES), 1)
    masks = (row == 0, row == SUBLANES - 1, col == 0, col == LANES - 1)

    def one_frame(f, carry):
        u = [quarters(low[f, i]) for i in range(width)]
        u = u + [quarters(rec[f, i]) for i in range(planes)]
        u = u + [quarters(high[f, i]) for i in range(width)]
        for sweep in range(width):
            u = relax(u, masks)
            extra = width - 1 - sweep
            if extra:
                u = (
                    [scaled(v, low_keep) for v in u[:extra]]
                    + u[extra : extra + planes]
                    + [scaled(v, high_keep) for v in u[extra + planes :]]
                )
        for i in range(planes):
            for z in range(2):
                for y in range(2):
                    at = pl.multiple_of(f * (planes * rows) + i * rows + z * SUBLANES, SUBLANES)
                    field[y, pl.ds(at, SUBLANES), :] = u[i][z][y].astype(BF16).astype(F32)
        return carry

    lax.fori_loop(0, frames, one_frame, 0)
    blocks = compact.shape[0]
    tiles = planes * rows * 2
    lane = iota((frames, LANES), 1)
    acc = jnp.zeros((frames, LANES), F32)
    for k in range(blocks):
        first, second, offset = split_run(starts[k], tiles)
        one = field[first & 1, pl.ds(first >> 1, frames, stride=planes * rows), :]
        two = field[second & 1, pl.ds(second >> 1, frames, stride=planes * rows), :]
        window = jnp.where(lane >= offset, one, two)
        voxel_windows[k] = window
        column = jnp.sum(window * compact[k : k + 1, :], axis=1, keepdims=True)
        acc = jnp.where(lane == k, column, acc)
    projected[...] = acc


def denoise_windows(starts, recording, low, high, compact):
    frames, planes, rows, _ = recording.shape
    blocks = compact.shape[0]
    return pl.pallas_call(
        denoise_kernel,
        in_specs=[SMEM, VMEM, VMEM, VMEM, VMEM],
        out_specs=[VMEM, VMEM],
        out_shape=[
            jax.ShapeDtypeStruct((blocks, frames, LANES), F32),
            jax.ShapeDtypeStruct((frames, LANES), F32),
        ],
        scratch_shapes=[pltpu.VMEM((2, frames * planes * rows, LANES), F32)],
        name="denoise",
    )(starts, recording, low, high, compact)


def combine_kernel(prior, labels, projected, corr, piece, slot_prior):
    owners = prior.shape[0]
    blocks = corr.shape[0]
    frames = projected.shape[0]
    span = owners * SUBLANES
    flat = prior[...].astype(F32).reshape(span, LANES).astype(BF16)
    owner = labels[:, 0:1]
    slot = labels[:, 1:2]
    source = iota((blocks, span), 1)
    pick = jnp.concatenate(
        [onehot(source == owner * SUBLANES + i) for i in range(SUBLANES)], axis=0
    )
    found = jnp.dot(pick, flat, preferred_element_type=F32)
    lane = iota((blocks, LANES), 1)
    wanted = (lane >= LANES // 2) & (lane % blocks == slot)
    parts = [
        jnp.where(wanted, found[i * blocks : (i + 1) * blocks], 0.0).astype(BF16)
        for i in range(SUBLANES)
    ]
    wide = SUBLANES * LANES
    here = iota((wide, LANES), 0)
    frame_of = (here // LANES) * 2 + (here % LANES - LANES // 2) // blocks
    frame_of = jnp.where(here % LANES >= LANES // 2, frame_of, -1)
    spread = onehot(frame_of == iota((wide, LANES), 1) % frames)
    earlier = jnp.dot(jnp.concatenate(parts, axis=1), spread, preferred_element_type=F32)
    slot_prior[...] = earlier
    repeat = jnp.where(
        iota((frames, LANES), 0) == iota((frames, LANES), 1) % frames, 1.0, 0.0
    )
    tiled = lax.dot_general(
        projected[...],
        repeat,
        (((0,), (0,)), ((), ())),
        precision=HIGHEST,
        preferred_element_type=F32,
    )[:blocks]
    value = tiled - jnp.dot(
        corr[:, :blocks], earlier, precision=HIGHEST, preferred_element_type=F32
    )
    row = iota((blocks, LANES), 0)
    value = jnp.where(lane // frames == row % SUBLANES, value, 0.0)
    lines = [
        jnp.sum(value[q * SUBLANES : (q + 1) * SUBLANES], axis=0, keepdims=True)
        for q in range(blocks // SUBLANES)
    ]
    terms = [two_terms(v) for v in lines]
    whole = jnp.concatenate([t[0] for t in terms] + [t[1] for t in terms], axis=0).astype(BF16)
    piece[...] = jnp.broadcast_to(whole[None], piece.shape)


def combine(prior, labels, projected, corr):
    blocks = corr.shape[0]
    return pl.pallas_call(
        combine_kernel,
        in_specs=[VMEM, VMEM, VMEM, VMEM],
        out_specs=[VMEM, VMEM],
        out_shape=[
            jax.ShapeDtypeStruct(prior.shape, BF16),
            jax.ShapeDtypeStruct((blocks, LANES), F32),
        ],
        name="combine",
    )(prior, labels, projected, corr)


def update_kernel(prior, gathered, labels, traces, slot_prior, voxel_windows, traces_new, sent):
    owners = prior.shape[0]
    blocks = slot_prior.shape[0]
    frames, owned = traces.shape
    span = owners * SUBLANES
    flat = prior[...].astype(F32).reshape(span, LANES).astype(BF16)
    values = gathered[...].astype(F32).reshape(span, LANES).astype(BF16)
    lead = 4 * SUBLANES
    picks = onehot(iota((lead, LANES), 0) == iota((lead, LANES), 1))
    lists = lax.dot_general(
        picks, flat, (((1,), (1,)), ((), ())), preferred_element_type=F32
    )
    comps = lists[:SUBLANES] * float(owned) + lists[SUBLANES : 2 * SUBLANES]
    diags = lists[2 * SUBLANES : 3 * SUBLANES]
    position = lax.axis_index("bricks")
    asked = labels[:, 0:1] * owned + labels[:, 1:2]
    held = position * owned + iota((owned, 1), 0)
    target = jnp.concatenate([asked, held], axis=0).astype(F32)
    count = blocks + owned
    matches = []
    weight = jnp.zeros((count, span), F32)
    for j in range(SUBLANES):
        match = comps[j : j + 1] == target
        matches.append(onehot(match))
        weight = weight + jnp.where(match, diags[j : j + 1], 0.0)
    weight = jnp.sum(weight, axis=1, keepdims=True)
    sums = jnp.dot(jnp.concatenate(matches, axis=0), values, preferred_element_type=F32)
    group = iota((count, LANES), 1) // frames
    total = jnp.zeros((count, LANES), F32)
    for j in range(SUBLANES):
        total = jnp.where(group == j, sums[j * count : (j + 1) * count], total)
    shift = LANES // 2
    while shift >= frames:
        total = total + pltpu.roll(total, shift, 1)
        shift //= 2
    repeat = onehot(iota((frames, LANES), 0) == iota((frames, LANES), 1) % frames)
    mine = lax.dot_general(
        traces[...], repeat, (((0,), (0,)), ((), ())), preferred_element_type=F32
    )
    before = jnp.concatenate([slot_prior[...], mine], axis=0)
    after = jnp.maximum(0.0, before + total / (weight + 1.0))
    padded = jnp.concatenate([after, jnp.zeros((LANES - count, LANES), F32)], axis=0)
    turned = padded.T
    traces_new[...] = turned[:frames, blocks:count]
    slots = turned[:frames].astype(BF16).astype(F32)
    lane = iota((SUBLANES, LANES), 1)
    packed = jnp.where(
        lane < blocks,
        slots[:SUBLANES],
        jnp.where(lane < 2 * blocks, pltpu.roll(slots[SUBLANES:], blocks, 1), 0.0),
    )
    for k in range(blocks):
        line = jnp.sum(voxel_windows[k] * slots[:, k : k + 1], axis=0, keepdims=True)
        for g in range(sent.shape[0]):
            sent[g, k : k + 1, :] = line
    for g in range(sent.shape[0]):
        sent[g, blocks : blocks + SUBLANES, :] = packed


def update(prior, gathered, labels, traces, slot_prior, voxel_windows, groups):
    blocks = slot_prior.shape[0]
    return pl.pallas_call(
        update_kernel,
        in_specs=[VMEM] * 6,
        out_specs=[VMEM, VMEM],
        out_shape=[
            jax.ShapeDtypeStruct(traces.shape, F32),
            jax.ShapeDtypeStruct((groups, blocks + SUBLANES, LANES), F32),
        ],
        name="update",
    )(prior, gathered, labels, traces, slot_prior, voxel_windows)


def finish_kernel(starts, shared, windows, compact, out):
    blocks, voxels = out.shape
    tiles = voxels // LANES
    groups = shared.shape[0]
    lane = iota((blocks, LANES), 1)
    row = iota((blocks, LANES), 0)
    out[...] = jnp.zeros(out.shape, out.dtype)
    product = shared[0, :blocks, :]
    for g in range(1, groups):
        product = product + shared[g, :blocks, :]
    slots = jnp.concatenate([shared[g, blocks:, :] for g in range(groups)], axis=0).astype(BF16)
    both = lax.dot_general(slots, slots, (((0,), (0,)), ((), ())), preferred_element_type=F32)
    gram = both[:blocks] + pltpu.roll(both[blocks : 2 * blocks], LANES - blocks, 1)
    norm = jnp.sum(jnp.where(lane == row, gram, 0.0), axis=1, keepdims=True) + 1.0
    spread = jnp.concatenate(
        [
            jnp.sum(windows[k].astype(F32) * gram[:, k : k + 1], axis=0, keepdims=True)
            for k in range(blocks)
        ],
        axis=0,
    )
    current = compact[...]
    stepped = jnp.maximum(current + (product - spread) / norm, 0.0)
    stepped = jnp.where(current > 0, stepped, 0.0)
    for k in range(blocks):
        first, second, offset = split_run(starts[k], tiles)
        for index, part in ((first, lane >= offset), (second, lane < offset)):
            at = lane_tile(index)
            old = out[:, at].astype(F32)
            out[:, at] = jnp.where((row == k) & part, stepped, old).astype(out.dtype)


def finish(starts, shared, windows, compact, voxels):
    blocks = windows.shape[0]
    return pl.pallas_call(
        finish_kernel,
        in_specs=[SMEM, VMEM, VMEM, VMEM],
        out_specs=VMEM,
        out_shape=jax.ShapeDtypeStruct((blocks, voxels), BF16),
        name="finish",
    )(starts, shared, windows, compact)


def halo_planes(recording, width):
    count = lax.axis_size("bricks")
    planes = recording.shape[1]
    tail = lax.slice_in_dim(recording, planes - width, planes, axis=1)
    head = lax.slice_in_dim(recording, 0, width, axis=1)
    low = lax.ppermute(tail, "bricks", [(i, i + 1) for i in range(count - 1)])
    high = lax.ppermute(head, "bricks", [(i + 1, i) for i in range(count - 1)])
    return low, high


def label_piece(traces, labels):
    blocks = labels.shape[0]
    lists = labels.T.reshape(2, blocks // SUBLANES, SUBLANES).astype(F32)
    lists = jnp.concatenate([lists, lists], axis=1)
    gap = jnp.zeros((SUBLANES, LANES // 2 - 2 * SUBLANES), F32)
    return jnp.concatenate(
        [lists[0], lists[1], gap, traces.astype(F32).reshape(SUBLANES, -1)], axis=1
    )


def shards(recording, traces, footprints, block_owner, block_slot):
    voxels = footprints.shape[1]
    owners = lax.axis_size("bricks")
    groups = lax.axis_size("frames")
    low, high = halo_planes(recording, 3)
    labels = jnp.concatenate([block_owner, block_slot[:, None]], axis=1)
    base = label_piece(traces, labels)
    starts, windows, compact, corr, piece = prepare(base, footprints, owners)
    prior = lax.all_to_all(piece, "bricks", 0, 0)
    voxel_windows, projected = denoise_windows(starts, recording, low, high, compact)
    partials, slot_prior = combine(prior, labels, projected, corr)
    gathered = lax.all_to_all(partials, "bricks", 0, 0)
    traces_new, sent = update(prior, gathered, labels, traces, slot_prior, voxel_windows, groups)
    shared = lax.all_to_all(sent, "frames", 0, 0)
    footprints_new = finish(starts, shared, windows, compact, voxels)
    return (traces_new, footprints_new)


def solution(mesh):
    return jax.shard_map(
        shards,
        mesh=mesh,
        in_specs=(
            P("frames", "bricks", None, None),
            P("frames", "bricks"),
            P("bricks", None),
            P("bricks", None),
            P("bricks"),
        ),
        out_specs=(P("frames", "bricks"), P("bricks", None)),
        check_vma=False,
    )
```

```python
import jax
import jax.numpy as jnp
from jax import lax
from jax.experimental import pallas as pl
from jax.experimental.pallas import tpu as pltpu
from jax.sharding import PartitionSpec as P


TIME_STEP = 0.14
HIGHEST = lax.Precision.HIGHEST
LANES = 128
SUBLANES = 8
F32 = jnp.float32
BF16 = jnp.bfloat16
VMEM = pl.BlockSpec(memory_space=pltpu.VMEM)
SMEM = pl.BlockSpec(memory_space=pltpu.SMEM)


def near(array):
    return pltpu.with_memory_space_constraint(array, pltpu.VMEM)


def near_scalar(array):
    return pltpu.with_memory_space_constraint(array, pltpu.SMEM)


def iota(shape, axis):
    return lax.broadcasted_iota(jnp.int32, shape, axis)


def onehot(mask):
    return jnp.where(mask, 1.0, 0.0).astype(BF16)


def split_run(start, tiles):
    first = start >> 7
    return first, (first + 1) & (tiles - 1), start & (LANES - 1)


def lane_tile(index):
    return pl.ds(pl.multiple_of(index * LANES, LANES), LANES)


def two_terms(value):
    high = value.astype(BF16).astype(F32)
    return high, value - high


def label_rows(owner, slot, traces):
    frames, owned = traces.shape
    blocks = owner.shape[1]
    lane = iota((1, LANES), 1)
    gap = jnp.zeros((1, LANES - blocks), F32)
    lists = [jnp.concatenate([x[...].astype(F32), gap], axis=1) for x in (owner, slot)]
    rows = []
    for q in range(blocks // SUBLANES):
        first = pltpu.roll(lists[0], (LANES - q * SUBLANES) % LANES, 1)
        second = pltpu.roll(lists[1], (LANES + SUBLANES - q * SUBLANES) % LANES, 1)
        rows.append(
            jnp.where(lane < SUBLANES, first, jnp.where(lane < 2 * SUBLANES, second, 0.0))
        )
    wide = jnp.concatenate(
        [traces[...].astype(F32), jnp.zeros((frames, LANES - owned), F32)], axis=1
    )
    lane = iota((SUBLANES, LANES), 1)
    half = LANES // 2
    moved = jnp.where(
        lane < half + owned,
        pltpu.roll(wide[:SUBLANES], half, 1),
        pltpu.roll(wide[SUBLANES:], half + owned, 1),
    )
    return jnp.concatenate(rows + rows, axis=0) + jnp.where(lane < half, 0.0, moved)


def prepare_kernel(owner, slot, traces, foot, starts, windows, compact, corr, piece):
    blocks, voxels = foot.shape
    tiles = voxels // LANES
    acc = jnp.zeros((blocks, LANES), BF16)
    for t in range(1, tiles):
        cell = foot[:, t * LANES : (t + 1) * LANES]
        acc = acc + jnp.where(cell > 0, jnp.asarray(t, BF16), jnp.asarray(0, BF16))
    tile_of = acc.astype(F32)
    lowest = jnp.min(tile_of, axis=1, keepdims=True)
    highest = jnp.max(tile_of, axis=1, keepdims=True)
    first_tile = jnp.where(highest - lowest > 1.5, highest, lowest)
    behind = jnp.sum(jnp.where(tile_of != first_tile, 1.0, 0.0), axis=1, keepdims=True)
    begin = (first_tile * LANES + behind).astype(jnp.int32)
    lane = iota((blocks, LANES), 1)
    row = iota((blocks, LANES), 0)
    sums = jnp.zeros((blocks, LANES), F32)
    for k in range(blocks):
        start = begin[k, 0]
        starts[k] = start
        first, second, offset = split_run(start, tiles)
        one = foot[:, lane_tile(first)].astype(F32)
        two = foot[:, lane_tile(second)].astype(F32)
        window = jnp.where(lane >= offset, one, two)
        windows[k] = window.astype(BF16)
        own = window[k : k + 1]
        compact[k : k + 1, :] = own
        sums = jnp.where(lane == k, jnp.sum(window * own, axis=1, keepdims=True), sums)
    corr[...] = sums
    diag = jnp.sum(jnp.where(lane == row, sums, 0.0), axis=1, keepdims=True)
    placed = jnp.where(lane == 2 * SUBLANES + row % SUBLANES, diag, 0.0)
    groups = blocks // SUBLANES
    rows = [
        jnp.sum(placed[q * SUBLANES : (q + 1) * SUBLANES], axis=0, keepdims=True)
        for q in range(groups)
    ]
    terms = [two_terms(r) for r in rows]
    part = jnp.concatenate([t[0] for t in terms] + [t[1] for t in terms], axis=0)
    whole = (label_rows(owner, slot, traces) + part).astype(BF16)
    piece[...] = jnp.broadcast_to(whole[None], piece.shape)


def prepare(owner, slot, traces, footprints, owners):
    blocks, _ = footprints.shape
    return pl.pallas_call(
        prepare_kernel,
        in_specs=[VMEM] * 4,
        out_specs=[SMEM, VMEM, VMEM, VMEM, VMEM],
        out_shape=[
            pltpu.SMEM((blocks,), jnp.int32),
            pltpu.VMEM((blocks, blocks, LANES), BF16),
            pltpu.VMEM((blocks, LANES), F32),
            pltpu.VMEM((blocks, LANES), F32),
            pltpu.VMEM((owners, SUBLANES, LANES), BF16),
        ],
        name="prepare",
    )(owner, slot, traces, footprints)


def flux_of(difference):
    return difference / (1.0 + difference * difference)


def relax(planes, masks):
    first_row, last_row, first_col, last_col = masks
    across = [
        [[flux_of(planes[i + 1][z][y] - planes[i][z][y]) for y in range(2)] for z in range(2)]
        for i in range(len(planes) - 1)
    ]
    out = []
    for i in range(1, len(planes) - 1):
        u = planes[i]
        edge = [[flux_of(u[0][0]), flux_of(u[0][1])], [flux_of(u[1][0]), None]]
        total = [[across[i][z][y] - across[i - 1][z][y] for y in range(2)] for z in range(2)]
        for y in range(2):
            low = pltpu.roll(u[0][y], SUBLANES - 1, 0)
            high = pltpu.roll(u[1][y], SUBLANES - 1, 0)
            down_low = flux_of(jnp.where(last_row, high, low) - u[0][y])
            down_high = flux_of(jnp.where(last_row, 0.0, high) - u[1][y])
            up_low = pltpu.roll(down_low, 1, 0)
            up_high = pltpu.roll(down_high, 1, 0)
            total[0][y] = total[0][y] + (down_low - jnp.where(first_row, edge[0][y], up_low))
            total[1][y] = total[1][y] + (down_high - jnp.where(first_row, up_low, up_high))
        for z in range(2):
            low = pltpu.roll(u[z][0], LANES - 1, 1)
            high = pltpu.roll(u[z][1], LANES - 1, 1)
            right_low = flux_of(jnp.where(last_col, high, low) - u[z][0])
            right_high = flux_of(jnp.where(last_col, 0.0, high) - u[z][1])
            left_low = pltpu.roll(right_low, 1, 1)
            left_high = pltpu.roll(right_high, 1, 1)
            total[z][0] = total[z][0] + (right_low - jnp.where(first_col, edge[z][0], left_low))
            total[z][1] = total[z][1] + (right_high - jnp.where(first_col, left_low, left_high))
        out.append([[u[z][y] + TIME_STEP * total[z][y] for y in range(2)] for z in range(2)])
    return out


def quarters(plane):
    wide = plane.astype(F32)
    return [
        [wide[z * SUBLANES : (z + 1) * SUBLANES, y * LANES : (y + 1) * LANES] for y in range(2)]
        for z in range(2)
    ]


def scaled(plane, keep):
    return [[cell * keep for cell in line] for line in plane]


def denoise_kernel(starts, rec, low, high, compact, voxel_windows, projected, field):
    frames, planes, rows, _ = rec.shape
    width = 3
    position = lax.axis_index("bricks")
    low_keep = jnp.where(position > 0, 1.0, 0.0)
    high_keep = jnp.where(position < lax.axis_size("bricks") - 1, 1.0, 0.0)
    row = iota((SUBLANES, LANES), 0)
    col = iota((SUBLANES, LANES), 1)
    masks = (row == 0, row == SUBLANES - 1, col == 0, col == LANES - 1)

    def one_frame(f, carry):
        u = [quarters(low[f, planes - width + i]) for i in range(width)]
        u = u + [quarters(rec[f, i]) for i in range(planes)]
        u = u + [quarters(high[f, i]) for i in range(width)]
        for sweep in range(width):
            u = relax(u, masks)
            extra = width - 1 - sweep
            if extra:
                u = (
                    [scaled(v, low_keep) for v in u[:extra]]
                    + u[extra : extra + planes]
                    + [scaled(v, high_keep) for v in u[extra + planes :]]
                )
        for i in range(planes):
            for z in range(2):
                for y in range(2):
                    at = pl.multiple_of(f * (planes * rows) + i * rows + z * SUBLANES, SUBLANES)
                    field[y, pl.ds(at, SUBLANES), :] = u[i][z][y].astype(BF16).astype(F32)
        return carry

    lax.fori_loop(0, frames, one_frame, 0)
    blocks = compact.shape[0]
    tiles = planes * rows * 2
    lane = iota((frames, LANES), 1)
    acc = jnp.zeros((frames, LANES), F32)
    for k in range(blocks):
        first, second, offset = split_run(starts[k], tiles)
        one = field[first & 1, pl.ds(first >> 1, frames, stride=planes * rows), :]
        two = field[second & 1, pl.ds(second >> 1, frames, stride=planes * rows), :]
        window = jnp.where(lane >= offset, one, two)
        voxel_windows[k] = window
        column = jnp.sum(window * compact[k : k + 1, :], axis=1, keepdims=True)
        acc = jnp.where(lane == k, column, acc)
    projected[...] = acc


def denoise_windows(starts, recording, low, high, compact):
    frames, planes, rows, _ = recording.shape
    blocks = compact.shape[0]
    return pl.pallas_call(
        denoise_kernel,
        in_specs=[SMEM, VMEM, VMEM, VMEM, VMEM],
        out_specs=[VMEM, VMEM],
        out_shape=[
            pltpu.VMEM((blocks, frames, LANES), F32),
            pltpu.VMEM((frames, LANES), F32),
        ],
        scratch_shapes=[pltpu.VMEM((2, frames * planes * rows, LANES), F32)],
        name="denoise",
    )(near_scalar(starts), recording, near(low), near(high), near(compact))


def as_column(line):
    count = line.shape[1]
    square = (count, count)
    same = iota(square, 0) == iota(square, 1)
    return jnp.sum(jnp.where(same, line, 0), axis=1, keepdims=True)


def combine_kernel(prior, owner, slot, projected, corr, piece, slot_prior):
    owners = prior.shape[0]
    blocks = corr.shape[0]
    frames = projected.shape[0]
    span = owners * SUBLANES
    flat = prior[...].astype(F32).reshape(span, LANES).astype(BF16)
    owner = as_column(owner[...])
    slot = as_column(slot[...])
    source = iota((blocks, span), 1)
    pick = jnp.concatenate(
        [onehot(source == owner * SUBLANES + i) for i in range(SUBLANES)], axis=0
    )
    found = jnp.dot(pick, flat, preferred_element_type=F32)
    lane = iota((blocks, LANES), 1)
    wanted = (lane >= LANES // 2) & (lane % blocks == slot)
    parts = [
        jnp.where(wanted, found[i * blocks : (i + 1) * blocks], 0.0).astype(BF16)
        for i in range(SUBLANES)
    ]
    wide = SUBLANES * LANES
    here = iota((wide, LANES), 0)
    frame_of = here // LANES + (here % LANES - LANES // 2) // blocks * SUBLANES
    frame_of = jnp.where(here % LANES >= LANES // 2, frame_of, -1)
    spread = onehot(frame_of == iota((wide, LANES), 1) % frames)
    earlier = jnp.dot(jnp.concatenate(parts, axis=1), spread, preferred_element_type=F32)
    slot_prior[...] = earlier
    repeat = jnp.where(
        iota((frames, LANES), 0) == iota((frames, LANES), 1) % frames, 1.0, 0.0
    )
    tiled = lax.dot_general(
        projected[...],
        repeat,
        (((0,), (0,)), ((), ())),
        precision=HIGHEST,
        preferred_element_type=F32,
    )[:blocks]
    value = tiled - jnp.dot(
        corr[:, :blocks], earlier, precision=HIGHEST, preferred_element_type=F32
    )
    row = iota((blocks, LANES), 0)
    value = jnp.where(lane // frames == row % SUBLANES, value, 0.0)
    lines = [
        jnp.sum(value[q * SUBLANES : (q + 1) * SUBLANES], axis=0, keepdims=True)
        for q in range(blocks // SUBLANES)
    ]
    terms = [two_terms(v) for v in lines]
    whole = jnp.concatenate([t[0] for t in terms] + [t[1] for t in terms], axis=0).astype(BF16)
    piece[...] = jnp.broadcast_to(whole[None], piece.shape)


def combine(prior, owner, slot, projected, corr):
    blocks = corr.shape[0]
    return pl.pallas_call(
        combine_kernel,
        in_specs=[VMEM] * 5,
        out_specs=[VMEM, VMEM],
        out_shape=[
            pltpu.VMEM(prior.shape, BF16),
            pltpu.VMEM((blocks, LANES), F32),
        ],
        name="combine",
    )(near(prior), owner, slot, near(projected), near(corr))


def update_kernel(
    prior, gathered, owner, slot, traces, slot_prior, voxel_windows, traces_new, sent
):
    owners = prior.shape[0]
    blocks = slot_prior.shape[0]
    frames, owned = traces.shape
    span = owners * SUBLANES
    flat = prior[...].astype(F32).reshape(span, LANES).astype(BF16)
    values = gathered[...].astype(F32).reshape(span, LANES).astype(BF16)
    lead = 4 * SUBLANES
    picks = onehot(iota((lead, LANES), 0) == iota((lead, LANES), 1))
    lists = lax.dot_general(
        picks, flat, (((1,), (1,)), ((), ())), preferred_element_type=F32
    )
    comps = lists[:SUBLANES] * float(owned) + lists[SUBLANES : 2 * SUBLANES]
    diags = lists[2 * SUBLANES : 3 * SUBLANES]
    position = lax.axis_index("bricks")
    asked = as_column(owner[...] * owned + slot[...])
    held = position * owned + iota((owned, 1), 0)
    target = jnp.concatenate([asked, held], axis=0).astype(F32)
    count = blocks + owned
    matches = []
    weight = jnp.zeros((count, span), F32)
    for j in range(SUBLANES):
        match = comps[j : j + 1] == target
        matches.append(onehot(match))
        weight = weight + jnp.where(match, diags[j : j + 1], 0.0)
    weight = jnp.sum(weight, axis=1, keepdims=True)
    sums = jnp.dot(jnp.concatenate(matches, axis=0), values, preferred_element_type=F32)
    group = iota((count, LANES), 1) // frames
    total = jnp.zeros((count, LANES), F32)
    for j in range(SUBLANES):
        total = jnp.where(group == j, sums[j * count : (j + 1) * count], total)
    shift = LANES // 2
    while shift >= frames:
        total = total + pltpu.roll(total, shift, 1)
        shift //= 2
    repeat = onehot(iota((frames, LANES), 0) == iota((frames, LANES), 1) % frames)
    mine = lax.dot_general(
        traces[...], repeat, (((0,), (0,)), ((), ())), preferred_element_type=F32
    )
    before = jnp.concatenate([slot_prior[...], mine], axis=0)
    after = jnp.maximum(0.0, before + total / (weight + 1.0))
    padded = jnp.concatenate([after, jnp.zeros((LANES - count, LANES), F32)], axis=0)
    turned = padded.T
    traces_new[...] = turned[:frames, blocks:count]
    slots = turned[:frames].astype(BF16).astype(F32)
    lane = iota((SUBLANES, LANES), 1)
    packed = jnp.where(
        lane < blocks,
        slots[:SUBLANES],
        jnp.where(lane < 2 * blocks, pltpu.roll(slots[SUBLANES:], blocks, 1), 0.0),
    )
    for k in range(blocks):
        line = jnp.sum(voxel_windows[k] * slots[:, k : k + 1], axis=0, keepdims=True)
        for g in range(sent.shape[0]):
            sent[g, k : k + 1, :] = line
    for g in range(sent.shape[0]):
        sent[g, blocks : blocks + SUBLANES, :] = packed


def update(prior, gathered, owner, slot, traces, slot_prior, voxel_windows, groups):
    blocks = slot_prior.shape[0]
    return pl.pallas_call(
        update_kernel,
        in_specs=[VMEM] * 7,
        out_specs=[VMEM, VMEM],
        out_shape=[
            jax.ShapeDtypeStruct(traces.shape, F32),
            pltpu.VMEM((groups, blocks + SUBLANES, LANES), F32),
        ],
        name="update",
    )(near(prior), near(gathered), owner, slot, traces, near(slot_prior), near(voxel_windows))


def finish_kernel(starts, shared, windows, compact, out):
    blocks, voxels = out.shape
    tiles = voxels // LANES
    groups = shared.shape[0]
    lane = iota((blocks, LANES), 1)
    row = iota((blocks, LANES), 0)
    out[...] = jnp.zeros(out.shape, out.dtype)
    product = shared[0, :blocks, :]
    for g in range(1, groups):
        product = product + shared[g, :blocks, :]
    slots = jnp.concatenate([shared[g, blocks:, :] for g in range(groups)], axis=0).astype(BF16)
    both = lax.dot_general(slots, slots, (((0,), (0,)), ((), ())), preferred_element_type=F32)
    gram = both[:blocks] + pltpu.roll(both[blocks : 2 * blocks], LANES - blocks, 1)
    norm = jnp.sum(jnp.where(lane == row, gram, 0.0), axis=1, keepdims=True) + 1.0
    spread = jnp.concatenate(
        [
            jnp.sum(windows[k].astype(F32) * gram[:, k : k + 1], axis=0, keepdims=True)
            for k in range(blocks)
        ],
        axis=0,
    )
    current = compact[...]
    stepped = jnp.maximum(current + (product - spread) / norm, 0.0)
    stepped = jnp.where(current > 0, stepped, 0.0)
    for k in range(blocks):
        first, second, offset = split_run(starts[k], tiles)
        for index, part in ((first, lane >= offset), (second, lane < offset)):
            at = lane_tile(index)
            old = out[:, at].astype(F32)
            out[:, at] = jnp.where((row == k) & part, stepped, old).astype(out.dtype)


def finish(starts, shared, windows, compact, voxels):
    blocks = windows.shape[0]
    return pl.pallas_call(
        finish_kernel,
        in_specs=[SMEM, VMEM, VMEM, VMEM],
        out_specs=VMEM,
        out_shape=jax.ShapeDtypeStruct((blocks, voxels), BF16),
        name="finish",
    )(near_scalar(starts), near(shared), near(windows), near(compact))


def halo_planes(recording):
    count = lax.axis_size("bricks")
    low = lax.ppermute(recording, "bricks", [(i, i + 1) for i in range(count - 1)])
    high = lax.ppermute(recording, "bricks", [(i + 1, i) for i in range(count - 1)])
    return low, high


def shards(recording, traces, footprints, block_owner, block_slot):
    voxels = footprints.shape[1]
    owners = lax.axis_size("bricks")
    groups = lax.axis_size("frames")
    low, high = halo_planes(recording)
    owner = block_owner.T
    slot = block_slot[None, :]
    starts, windows, compact, corr, piece = prepare(owner, slot, traces, footprints, owners)
    prior = lax.all_to_all(piece, "bricks", 0, 0)
    voxel_windows, projected = denoise_windows(starts, recording, low, high, compact)
    partials, slot_prior = combine(prior, owner, slot, projected, corr)
    gathered = lax.all_to_all(partials, "bricks", 0, 0)
    traces_new, sent = update(
        prior, gathered, owner, slot, traces, slot_prior, voxel_windows, groups
    )
    shared = lax.all_to_all(sent, "frames", 0, 0)
    footprints_new = finish(starts, shared, windows, compact, voxels)
    return (traces_new, footprints_new)


def solution(mesh):
    return jax.shard_map(
        shards,
        mesh=mesh,
        in_specs=(
            P("frames", "bricks", None, None),
            P("frames", "bricks"),
            P("bricks", None),
            P("bricks", None),
            P("bricks"),
        ),
        out_specs=(P("frames", "bricks"), P("bricks", None)),
        check_vma=False,
    )
```

```python
import jax
import jax.numpy as jnp
from jax import lax
from jax.experimental import pallas as pl
from jax.experimental.pallas import tpu as pltpu
from jax.sharding import PartitionSpec as P


TIME_STEP = 0.14
HIGHEST = lax.Precision.HIGHEST
LANES = 128
SUBLANES = 8
F32 = jnp.float32
BF16 = jnp.bfloat16
VMEM = pl.BlockSpec(memory_space=pltpu.VMEM)
SMEM = pl.BlockSpec(memory_space=pltpu.SMEM)
PARAMS = pltpu.CompilerParams(vmem_limit_bytes=16 * 2**20)


def near(array):
    return pltpu.with_memory_space_constraint(array, pltpu.VMEM)


def near_scalar(array):
    return pltpu.with_memory_space_constraint(array, pltpu.SMEM)


def iota(shape, axis):
    return lax.broadcasted_iota(jnp.int32, shape, axis)


def onehot(mask):
    return jnp.where(mask, 1.0, 0.0).astype(BF16)


def split_run(start, tiles):
    first = start >> 7
    return first, (first + 1) & (tiles - 1), start & (LANES - 1)


def lane_tile(index):
    return pl.ds(pl.multiple_of(index * LANES, LANES), LANES)


def two_terms(value):
    high = value.astype(BF16).astype(F32)
    return high, value - high


def label_rows(owner, slot, traces):
    frames, owned = traces.shape
    blocks = owner.shape[1]
    lane = iota((1, LANES), 1)
    gap = jnp.zeros((1, LANES - blocks), F32)
    lists = [jnp.concatenate([x[...].astype(F32), gap], axis=1) for x in (owner, slot)]
    rows = []
    for q in range(blocks // SUBLANES):
        first = pltpu.roll(lists[0], (LANES - q * SUBLANES) % LANES, 1)
        second = pltpu.roll(lists[1], (LANES + SUBLANES - q * SUBLANES) % LANES, 1)
        rows.append(
            jnp.where(lane < SUBLANES, first, jnp.where(lane < 2 * SUBLANES, second, 0.0))
        )
    wide = jnp.concatenate(
        [traces[...].astype(F32), jnp.zeros((frames, LANES - owned), F32)], axis=1
    )
    lane = iota((SUBLANES, LANES), 1)
    half = LANES // 2
    moved = jnp.where(
        lane < half + owned,
        pltpu.roll(wide[:SUBLANES], half, 1),
        pltpu.roll(wide[SUBLANES:], half + owned, 1),
    )
    return jnp.concatenate(rows + rows, axis=0) + jnp.where(lane < half, 0.0, moved)


def prepare_kernel(owner, slot, traces, foot, starts, windows, compact, corr, piece):
    blocks, voxels = foot.shape
    tiles = voxels // LANES
    acc = jnp.zeros((blocks, LANES), BF16)
    for t in range(1, tiles):
        cell = foot[:, t * LANES : (t + 1) * LANES]
        acc = acc + jnp.where(cell > 0, jnp.asarray(t, BF16), jnp.asarray(0, BF16))
    tile_of = acc.astype(F32)
    lowest = jnp.min(tile_of, axis=1, keepdims=True)
    highest = jnp.max(tile_of, axis=1, keepdims=True)
    first_tile = jnp.where(highest - lowest > 1.5, highest, lowest)
    behind = jnp.sum(jnp.where(tile_of != first_tile, 1.0, 0.0), axis=1, keepdims=True)
    begin = (first_tile * LANES + behind).astype(jnp.int32)
    lane = iota((blocks, LANES), 1)
    row = iota((blocks, LANES), 0)
    sums = jnp.zeros((blocks, LANES), F32)
    for k in range(blocks):
        start = begin[k, 0]
        starts[k] = start
        first, second, offset = split_run(start, tiles)
        one = foot[:, lane_tile(first)].astype(F32)
        two = foot[:, lane_tile(second)].astype(F32)
        window = jnp.where(lane >= offset, one, two)
        windows[k] = window.astype(BF16)
        own = window[k : k + 1]
        compact[k : k + 1, :] = own
        sums = jnp.where(lane == k, jnp.sum(window * own, axis=1, keepdims=True), sums)
    corr[...] = sums
    diag = jnp.sum(jnp.where(lane == row, sums, 0.0), axis=1, keepdims=True)
    placed = jnp.where(lane == 2 * SUBLANES + row % SUBLANES, diag, 0.0)
    groups = blocks // SUBLANES
    rows = [
        jnp.sum(placed[q * SUBLANES : (q + 1) * SUBLANES], axis=0, keepdims=True)
        for q in range(groups)
    ]
    terms = [two_terms(r) for r in rows]
    part = jnp.concatenate([t[0] for t in terms] + [t[1] for t in terms], axis=0)
    whole = (label_rows(owner, slot, traces) + part).astype(BF16)
    piece[...] = jnp.broadcast_to(whole[None], piece.shape)


def prepare(owner, slot, traces, footprints, owners):
    blocks, _ = footprints.shape
    return pl.pallas_call(
        prepare_kernel,
        in_specs=[VMEM] * 4,
        out_specs=[SMEM, VMEM, VMEM, VMEM, VMEM],
        out_shape=[
            pltpu.SMEM((blocks,), jnp.int32),
            pltpu.VMEM((blocks, blocks, LANES), BF16),
            pltpu.VMEM((blocks, LANES), F32),
            pltpu.VMEM((blocks, LANES), F32),
            pltpu.VMEM((owners, SUBLANES, LANES), BF16),
        ],
        compiler_params=PARAMS,
        name="prepare",
    )(near(owner), near(slot), near(traces), near(footprints))


def flux_of(difference):
    return difference / (1.0 + difference * difference)


def relax(planes, masks):
    first_row, last_row, first_col, last_col = masks
    across = [
        [[flux_of(planes[i + 1][z][y] - planes[i][z][y]) for y in range(2)] for z in range(2)]
        for i in range(len(planes) - 1)
    ]
    out = []
    for i in range(1, len(planes) - 1):
        u = planes[i]
        edge = [[flux_of(u[0][0]), flux_of(u[0][1])], [flux_of(u[1][0]), None]]
        total = [[across[i][z][y] - across[i - 1][z][y] for y in range(2)] for z in range(2)]
        for y in range(2):
            low = pltpu.roll(u[0][y], SUBLANES - 1, 0)
            high = pltpu.roll(u[1][y], SUBLANES - 1, 0)
            down_low = flux_of(jnp.where(last_row, high, low) - u[0][y])
            down_high = flux_of(jnp.where(last_row, 0.0, high) - u[1][y])
            up_low = pltpu.roll(down_low, 1, 0)
            up_high = pltpu.roll(down_high, 1, 0)
            total[0][y] = total[0][y] + (down_low - jnp.where(first_row, edge[0][y], up_low))
            total[1][y] = total[1][y] + (down_high - jnp.where(first_row, up_low, up_high))
        for z in range(2):
            low = pltpu.roll(u[z][0], LANES - 1, 1)
            high = pltpu.roll(u[z][1], LANES - 1, 1)
            right_low = flux_of(jnp.where(last_col, high, low) - u[z][0])
            right_high = flux_of(jnp.where(last_col, 0.0, high) - u[z][1])
            left_low = pltpu.roll(right_low, 1, 1)
            left_high = pltpu.roll(right_high, 1, 1)
            total[z][0] = total[z][0] + (right_low - jnp.where(first_col, edge[z][0], left_low))
            total[z][1] = total[z][1] + (right_high - jnp.where(first_col, left_low, left_high))
        out.append([[u[z][y] + TIME_STEP * total[z][y] for y in range(2)] for z in range(2)])
    return out


def quarters(plane):
    wide = plane.astype(F32)
    return [
        [wide[z * SUBLANES : (z + 1) * SUBLANES, y * LANES : (y + 1) * LANES] for y in range(2)]
        for z in range(2)
    ]


def scaled(plane, keep):
    return [[cell * keep for cell in line] for line in plane]


def denoise_kernel(starts, rec, low, high, compact, voxel_windows, projected, field):
    frames, planes, rows, _ = rec.shape
    width = 3
    position = lax.axis_index("bricks")
    low_keep = jnp.where(position > 0, 1.0, 0.0)
    high_keep = jnp.where(position < lax.axis_size("bricks") - 1, 1.0, 0.0)
    row = iota((SUBLANES, LANES), 0)
    col = iota((SUBLANES, LANES), 1)
    masks = (row == 0, row == SUBLANES - 1, col == 0, col == LANES - 1)

    def one_frame(f, carry):
        u = [quarters(low[f, planes - width + i]) for i in range(width)]
        u = u + [quarters(rec[f, i]) for i in range(planes)]
        u = u + [quarters(high[f, i]) for i in range(width)]
        for sweep in range(width):
            u = relax(u, masks)
            extra = width - 1 - sweep
            if extra:
                u = (
                    [scaled(v, low_keep) for v in u[:extra]]
                    + u[extra : extra + planes]
                    + [scaled(v, high_keep) for v in u[extra + planes :]]
                )
        for i in range(planes):
            for z in range(2):
                for y in range(2):
                    at = pl.multiple_of(f * (planes * rows) + i * rows + z * SUBLANES, SUBLANES)
                    field[y, pl.ds(at, SUBLANES), :] = u[i][z][y].astype(BF16).astype(F32)
        return carry

    lax.fori_loop(0, frames, one_frame, 0)
    blocks = compact.shape[0]
    tiles = planes * rows * 2
    lane = iota((frames, LANES), 1)
    acc = jnp.zeros((frames, LANES), F32)
    for k in range(blocks):
        first, second, offset = split_run(starts[k], tiles)
        one = field[first & 1, pl.ds(first >> 1, frames, stride=planes * rows), :]
        two = field[second & 1, pl.ds(second >> 1, frames, stride=planes * rows), :]
        window = jnp.where(lane >= offset, one, two)
        voxel_windows[k] = window
        column = jnp.sum(window * compact[k : k + 1, :], axis=1, keepdims=True)
        acc = jnp.where(lane == k, column, acc)
    projected[...] = acc


def denoise_windows(starts, recording, low, high, compact):
    frames, planes, rows, _ = recording.shape
    blocks = compact.shape[0]
    return pl.pallas_call(
        denoise_kernel,
        in_specs=[SMEM, VMEM, VMEM, VMEM, VMEM],
        out_specs=[VMEM, VMEM],
        out_shape=[
            pltpu.VMEM((blocks, frames, LANES), F32),
            pltpu.VMEM((frames, LANES), F32),
        ],
        scratch_shapes=[pltpu.VMEM((2, frames * planes * rows, LANES), F32)],
        compiler_params=PARAMS,
        name="denoise",
    )(near_scalar(starts), near(recording), near(low), near(high), near(compact))


def as_column(line):
    count = line.shape[1]
    square = (count, count)
    same = iota(square, 0) == iota(square, 1)
    return jnp.sum(jnp.where(same, line, 0), axis=1, keepdims=True)


def combine_kernel(prior, owner, slot, projected, corr, piece, slot_prior):
    owners = prior.shape[0]
    blocks = corr.shape[0]
    frames = projected.shape[0]
    span = owners * SUBLANES
    flat = prior[...].astype(F32).reshape(span, LANES).astype(BF16)
    owner = as_column(owner[...])
    slot = as_column(slot[...])
    source = iota((blocks, span), 1)
    pick = jnp.concatenate(
        [onehot(source == owner * SUBLANES + i) for i in range(SUBLANES)], axis=0
    )
    found = jnp.dot(pick, flat, preferred_element_type=F32)
    lane = iota((blocks, LANES), 1)
    wanted = (lane >= LANES // 2) & (lane % blocks == slot)
    parts = [
        jnp.where(wanted, found[i * blocks : (i + 1) * blocks], 0.0).astype(BF16)
        for i in range(SUBLANES)
    ]
    wide = SUBLANES * LANES
    here = iota((wide, LANES), 0)
    frame_of = here // LANES + (here % LANES - LANES // 2) // blocks * SUBLANES
    frame_of = jnp.where(here % LANES >= LANES // 2, frame_of, -1)
    spread = onehot(frame_of == iota((wide, LANES), 1) % frames)
    earlier = jnp.dot(jnp.concatenate(parts, axis=1), spread, preferred_element_type=F32)
    slot_prior[...] = earlier
    repeat = jnp.where(
        iota((frames, LANES), 0) == iota((frames, LANES), 1) % frames, 1.0, 0.0
    )
    tiled = lax.dot_general(
        projected[...],
        repeat,
        (((0,), (0,)), ((), ())),
        precision=HIGHEST,
        preferred_element_type=F32,
    )[:blocks]
    value = tiled - jnp.dot(
        corr[:, :blocks], earlier, precision=HIGHEST, preferred_element_type=F32
    )
    row = iota((blocks, LANES), 0)
    value = jnp.where(lane // frames == row % SUBLANES, value, 0.0)
    lines = [
        jnp.sum(value[q * SUBLANES : (q + 1) * SUBLANES], axis=0, keepdims=True)
        for q in range(blocks // SUBLANES)
    ]
    terms = [two_terms(v) for v in lines]
    whole = jnp.concatenate([t[0] for t in terms] + [t[1] for t in terms], axis=0).astype(BF16)
    piece[...] = jnp.broadcast_to(whole[None], piece.shape)


def combine(prior, owner, slot, projected, corr):
    blocks = corr.shape[0]
    return pl.pallas_call(
        combine_kernel,
        in_specs=[VMEM] * 5,
        out_specs=[VMEM, VMEM],
        out_shape=[
            pltpu.VMEM(prior.shape, BF16),
            pltpu.VMEM((blocks, LANES), F32),
        ],
        compiler_params=PARAMS,
        name="combine",
    )(near(prior), near(owner), near(slot), near(projected), near(corr))


def update_kernel(
    prior, gathered, owner, slot, traces, slot_prior, voxel_windows, traces_new, sent
):
    owners = prior.shape[0]
    blocks = slot_prior.shape[0]
    frames, owned = traces.shape
    span = owners * SUBLANES
    flat = prior[...].astype(F32).reshape(span, LANES).astype(BF16)
    values = gathered[...].astype(F32).reshape(span, LANES).astype(BF16)
    lead = 4 * SUBLANES
    picks = onehot(iota((lead, LANES), 0) == iota((lead, LANES), 1))
    lists = lax.dot_general(
        picks, flat, (((1,), (1,)), ((), ())), preferred_element_type=F32
    )
    comps = lists[:SUBLANES] * float(owned) + lists[SUBLANES : 2 * SUBLANES]
    diags = lists[2 * SUBLANES : 3 * SUBLANES]
    position = lax.axis_index("bricks")
    asked = as_column(owner[...] * owned + slot[...])
    held = position * owned + iota((owned, 1), 0)
    target = jnp.concatenate([asked, held], axis=0).astype(F32)
    count = blocks + owned
    matches = []
    weight = jnp.zeros((count, span), F32)
    for j in range(SUBLANES):
        match = comps[j : j + 1] == target
        matches.append(onehot(match))
        weight = weight + jnp.where(match, diags[j : j + 1], 0.0)
    weight = jnp.sum(weight, axis=1, keepdims=True)
    sums = jnp.dot(jnp.concatenate(matches, axis=0), values, preferred_element_type=F32)
    group = iota((count, LANES), 1) // frames
    total = jnp.zeros((count, LANES), F32)
    for j in range(SUBLANES):
        total = jnp.where(group == j, sums[j * count : (j + 1) * count], total)
    shift = LANES // 2
    while shift >= frames:
        total = total + pltpu.roll(total, shift, 1)
        shift //= 2
    repeat = onehot(iota((frames, LANES), 0) == iota((frames, LANES), 1) % frames)
    mine = lax.dot_general(
        traces[...], repeat, (((0,), (0,)), ((), ())), preferred_element_type=F32
    )
    before = jnp.concatenate([slot_prior[...], mine], axis=0)
    after = jnp.maximum(0.0, before + total / (weight + 1.0))
    padded = jnp.concatenate([after, jnp.zeros((LANES - count, LANES), F32)], axis=0)
    turned = padded.T
    traces_new[...] = turned[:frames, blocks:count]
    slots = turned[:frames].astype(BF16).astype(F32)
    lane = iota((SUBLANES, LANES), 1)
    packed = jnp.where(
        lane < blocks,
        slots[:SUBLANES],
        jnp.where(lane < 2 * blocks, pltpu.roll(slots[SUBLANES:], blocks, 1), 0.0),
    )
    for k in range(blocks):
        line = jnp.sum(voxel_windows[k] * slots[:, k : k + 1], axis=0, keepdims=True)
        for g in range(sent.shape[0]):
            sent[g, k : k + 1, :] = line
    for g in range(sent.shape[0]):
        sent[g, blocks : blocks + SUBLANES, :] = packed


def update(prior, gathered, owner, slot, traces, slot_prior, voxel_windows, groups):
    blocks = slot_prior.shape[0]
    return pl.pallas_call(
        update_kernel,
        in_specs=[VMEM] * 7,
        out_specs=[VMEM, VMEM],
        out_shape=[
            pltpu.VMEM(traces.shape, F32),
            pltpu.VMEM((groups, blocks + SUBLANES, LANES), F32),
        ],
        compiler_params=PARAMS,
        name="update",
    )(
        near(prior),
        near(gathered),
        near(owner),
        near(slot),
        near(traces),
        near(slot_prior),
        near(voxel_windows),
    )


def finish_kernel(starts, shared, windows, compact, fresh, out, traces_new):
    traces_new[...] = fresh[...]
    blocks, voxels = out.shape
    tiles = voxels // LANES
    groups = shared.shape[0]
    lane = iota((blocks, LANES), 1)
    row = iota((blocks, LANES), 0)
    out[...] = jnp.zeros(out.shape, out.dtype)
    product = shared[0, :blocks, :]
    for g in range(1, groups):
        product = product + shared[g, :blocks, :]
    slots = jnp.concatenate([shared[g, blocks:, :] for g in range(groups)], axis=0).astype(BF16)
    both = lax.dot_general(slots, slots, (((0,), (0,)), ((), ())), preferred_element_type=F32)
    gram = both[:blocks] + pltpu.roll(both[blocks : 2 * blocks], LANES - blocks, 1)
    norm = jnp.sum(jnp.where(lane == row, gram, 0.0), axis=1, keepdims=True) + 1.0
    spread = jnp.concatenate(
        [
            jnp.sum(windows[k].astype(F32) * gram[:, k : k + 1], axis=0, keepdims=True)
            for k in range(blocks)
        ],
        axis=0,
    )
    current = compact[...]
    stepped = jnp.maximum(current + (product - spread) / norm, 0.0)
    stepped = jnp.where(current > 0, stepped, 0.0)
    for k in range(blocks):
        first, second, offset = split_run(starts[k], tiles)
        for index, part in ((first, lane >= offset), (second, lane < offset)):
            at = lane_tile(index)
            old = out[:, at].astype(F32)
            out[:, at] = jnp.where((row == k) & part, stepped, old).astype(out.dtype)


def finish(starts, shared, windows, compact, fresh, voxels):
    blocks = windows.shape[0]
    return pl.pallas_call(
        finish_kernel,
        in_specs=[SMEM, VMEM, VMEM, VMEM, VMEM],
        out_specs=[VMEM, VMEM],
        out_shape=[
            jax.ShapeDtypeStruct((blocks, voxels), BF16),
            jax.ShapeDtypeStruct(fresh.shape, fresh.dtype),
        ],
        compiler_params=PARAMS,
        name="finish",
    )(near_scalar(starts), near(shared), near(windows), near(compact), near(fresh))


def halo_planes(recording):
    count = lax.axis_size("bricks")
    low = lax.ppermute(recording, "bricks", [(i, i + 1) for i in range(count - 1)])
    high = lax.ppermute(recording, "bricks", [(i + 1, i) for i in range(count - 1)])
    return low, high


def shards(recording, traces, footprints, block_owner, block_slot):
    voxels = footprints.shape[1]
    owners = lax.axis_size("bricks")
    groups = lax.axis_size("frames")
    low, high = halo_planes(recording)
    owner = block_owner.T
    slot = block_slot[None, :]
    starts, windows, compact, corr, piece = prepare(owner, slot, traces, footprints, owners)
    prior = lax.all_to_all(piece, "bricks", 0, 0)
    voxel_windows, projected = denoise_windows(starts, recording, low, high, compact)
    partials, slot_prior = combine(prior, owner, slot, projected, corr)
    gathered = lax.all_to_all(partials, "bricks", 0, 0)
    fresh, sent = update(prior, gathered, owner, slot, traces, slot_prior, voxel_windows, groups)
    shared = lax.all_to_all(sent, "frames", 0, 0)
    footprints_new, traces_new = finish(starts, shared, windows, compact, fresh, voxels)
    return (traces_new, footprints_new)


def solution(mesh):
    return jax.shard_map(
        shards,
        mesh=mesh,
        in_specs=(
            P("frames", "bricks", None, None),
            P("frames", "bricks"),
            P("bricks", None),
            P("bricks", None),
            P("bricks"),
        ),
        out_specs=(P("frames", "bricks"), P("bricks", None)),
        check_vma=False,
    )
```

```python
import jax
import jax.numpy as jnp
from jax import lax
from jax.experimental import pallas as pl
from jax.experimental.pallas import tpu as pltpu
from jax.sharding import PartitionSpec as P


TIME_STEP = 0.14
HIGHEST = lax.Precision.HIGHEST
LANES = 128
SUBLANES = 8
F32 = jnp.float32
BF16 = jnp.bfloat16
VMEM = pl.BlockSpec(memory_space=pltpu.VMEM)
SMEM = pl.BlockSpec(memory_space=pltpu.SMEM)
PARAMS = pltpu.CompilerParams(vmem_limit_bytes=16 * 2**20)


def near(array):
    return pltpu.with_memory_space_constraint(array, pltpu.VMEM)


def far(array):
    return pltpu.with_memory_space_constraint(array, pltpu.HBM)


def near_scalar(array):
    return pltpu.with_memory_space_constraint(array, pltpu.SMEM)


def iota(shape, axis):
    return lax.broadcasted_iota(jnp.int32, shape, axis)


def onehot(mask):
    return jnp.where(mask, 1.0, 0.0).astype(BF16)


def split_run(start, tiles):
    first = start >> 7
    return first, (first + 1) & (tiles - 1), start & (LANES - 1)


def lane_tile(index):
    return pl.ds(pl.multiple_of(index * LANES, LANES), LANES)


def two_terms(value):
    high = value.astype(BF16).astype(F32)
    return high, value - high


def label_rows(owner, slot, traces):
    frames, owned = traces.shape
    blocks = owner.shape[1]
    lane = iota((1, LANES), 1)
    gap = jnp.zeros((1, LANES - blocks), F32)
    lists = [jnp.concatenate([x[...].astype(F32), gap], axis=1) for x in (owner, slot)]
    rows = []
    for q in range(blocks // SUBLANES):
        first = pltpu.roll(lists[0], (LANES - q * SUBLANES) % LANES, 1)
        second = pltpu.roll(lists[1], (LANES + SUBLANES - q * SUBLANES) % LANES, 1)
        rows.append(
            jnp.where(lane < SUBLANES, first, jnp.where(lane < 2 * SUBLANES, second, 0.0))
        )
    wide = jnp.concatenate(
        [traces[...].astype(F32), jnp.zeros((frames, LANES - owned), F32)], axis=1
    )
    lane = iota((SUBLANES, LANES), 1)
    half = LANES // 2
    moved = jnp.where(
        lane < half + owned,
        pltpu.roll(wide[:SUBLANES], half, 1),
        pltpu.roll(wide[SUBLANES:], half + owned, 1),
    )
    return jnp.concatenate(rows + rows, axis=0) + jnp.where(lane < half, 0.0, moved)


def prepare_kernel(owner, slot, traces, foot, starts, windows, compact, corr, piece):
    blocks, voxels = foot.shape
    tiles = voxels // LANES
    acc = jnp.zeros((blocks, LANES), BF16)
    for t in range(1, tiles):
        cell = foot[:, t * LANES : (t + 1) * LANES]
        acc = acc + jnp.where(cell > 0, jnp.asarray(t, BF16), jnp.asarray(0, BF16))
    tile_of = acc.astype(F32)
    lowest = jnp.min(tile_of, axis=1, keepdims=True)
    highest = jnp.max(tile_of, axis=1, keepdims=True)
    first_tile = jnp.where(highest - lowest > 1.5, highest, lowest)
    behind = jnp.sum(jnp.where(tile_of != first_tile, 1.0, 0.0), axis=1, keepdims=True)
    begin = (first_tile * LANES + behind).astype(jnp.int32)
    lane = iota((blocks, LANES), 1)
    row = iota((blocks, LANES), 0)
    sums = jnp.zeros((blocks, LANES), F32)
    for k in range(blocks):
        start = begin[k, 0]
        starts[k] = start
        first, second, offset = split_run(start, tiles)
        one = foot[:, lane_tile(first)].astype(F32)
        two = foot[:, lane_tile(second)].astype(F32)
        window = jnp.where(lane >= offset, one, two)
        windows[k] = window.astype(BF16)
        own = window[k : k + 1]
        compact[k : k + 1, :] = own
        sums = jnp.where(lane == k, jnp.sum(window * own, axis=1, keepdims=True), sums)
    corr[...] = sums
    diag = jnp.sum(jnp.where(lane == row, sums, 0.0), axis=1, keepdims=True)
    placed = jnp.where(lane == 2 * SUBLANES + row % SUBLANES, diag, 0.0)
    groups = blocks // SUBLANES
    rows = [
        jnp.sum(placed[q * SUBLANES : (q + 1) * SUBLANES], axis=0, keepdims=True)
        for q in range(groups)
    ]
    terms = [two_terms(r) for r in rows]
    part = jnp.concatenate([t[0] for t in terms] + [t[1] for t in terms], axis=0)
    whole = (label_rows(owner, slot, traces) + part).astype(BF16)
    piece[...] = jnp.broadcast_to(whole[None], piece.shape)


def prepare(owner, slot, traces, footprints, owners):
    blocks, _ = footprints.shape
    return pl.pallas_call(
        prepare_kernel,
        in_specs=[VMEM] * 4,
        out_specs=[SMEM, VMEM, VMEM, VMEM, VMEM],
        out_shape=[
            pltpu.SMEM((blocks,), jnp.int32),
            pltpu.VMEM((blocks, blocks, LANES), BF16),
            pltpu.VMEM((blocks, LANES), F32),
            pltpu.VMEM((blocks, LANES), F32),
            pltpu.VMEM((owners, SUBLANES, LANES), BF16),
        ],
        compiler_params=PARAMS,
        name="prepare",
    )(far(owner), far(slot), far(traces), far(footprints))


def flux_of(difference):
    return difference / (1.0 + difference * difference)


def relax(planes, masks):
    first_row, last_row, first_col, last_col = masks
    across = [
        [[flux_of(planes[i + 1][z][y] - planes[i][z][y]) for y in range(2)] for z in range(2)]
        for i in range(len(planes) - 1)
    ]
    out = []
    for i in range(1, len(planes) - 1):
        u = planes[i]
        edge = [[flux_of(u[0][0]), flux_of(u[0][1])], [flux_of(u[1][0]), None]]
        total = [[across[i][z][y] - across[i - 1][z][y] for y in range(2)] for z in range(2)]
        for y in range(2):
            low = pltpu.roll(u[0][y], SUBLANES - 1, 0)
            high = pltpu.roll(u[1][y], SUBLANES - 1, 0)
            down_low = flux_of(jnp.where(last_row, high, low) - u[0][y])
            down_high = flux_of(jnp.where(last_row, 0.0, high) - u[1][y])
            up_low = pltpu.roll(down_low, 1, 0)
            up_high = pltpu.roll(down_high, 1, 0)
            total[0][y] = total[0][y] + (down_low - jnp.where(first_row, edge[0][y], up_low))
            total[1][y] = total[1][y] + (down_high - jnp.where(first_row, up_low, up_high))
        for z in range(2):
            low = pltpu.roll(u[z][0], LANES - 1, 1)
            high = pltpu.roll(u[z][1], LANES - 1, 1)
            right_low = flux_of(jnp.where(last_col, high, low) - u[z][0])
            right_high = flux_of(jnp.where(last_col, 0.0, high) - u[z][1])
            left_low = pltpu.roll(right_low, 1, 1)
            left_high = pltpu.roll(right_high, 1, 1)
            total[z][0] = total[z][0] + (right_low - jnp.where(first_col, edge[z][0], left_low))
            total[z][1] = total[z][1] + (right_high - jnp.where(first_col, left_low, left_high))
        out.append([[u[z][y] + TIME_STEP * total[z][y] for y in range(2)] for z in range(2)])
    return out


def quarters(plane):
    wide = plane.astype(F32)
    return [
        [wide[z * SUBLANES : (z + 1) * SUBLANES, y * LANES : (y + 1) * LANES] for y in range(2)]
        for z in range(2)
    ]


def scaled(plane, keep):
    return [[cell * keep for cell in line] for line in plane]


def denoise_kernel(starts, rec, pair, other, compact, voxel_windows, projected, field):
    frames, planes, rows, _ = rec.shape
    width = 3
    position = lax.axis_index("bricks")
    low_keep = jnp.where(position > 0, 1.0, 0.0)
    high_keep = jnp.where(position < lax.axis_size("bricks") - 1, 1.0, 0.0)
    row = iota((SUBLANES, LANES), 0)
    col = iota((SUBLANES, LANES), 1)
    masks = (row == 0, row == SUBLANES - 1, col == 0, col == LANES - 1)

    def one_frame(f, low, high):
        u = [quarters(low[f, planes - width + i]) for i in range(width)]
        u = u + [quarters(rec[f, i]) for i in range(planes)]
        u = u + [quarters(high[f, i]) for i in range(width)]
        for sweep in range(width):
            u = relax(u, masks)
            extra = width - 1 - sweep
            if extra:
                u = (
                    [scaled(v, low_keep) for v in u[:extra]]
                    + u[extra : extra + planes]
                    + [scaled(v, high_keep) for v in u[extra + planes :]]
                )
        for i in range(planes):
            for z in range(2):
                for y in range(2):
                    at = pl.multiple_of(f * (planes * rows) + i * rows + z * SUBLANES, SUBLANES)
                    field[y, pl.ds(at, SUBLANES), :] = u[i][z][y].astype(BF16).astype(F32)

    odd = position % 2 == 1
    for is_odd, low, high in ((True, pair, other), (False, other, pair)):

        @pl.when(odd if is_odd else jnp.logical_not(odd))
        def _(low=low, high=high):
            pl.loop(0, frames)(lambda f: one_frame(f, low, high))

    blocks = compact.shape[0]
    tiles = planes * rows * 2
    lane = iota((frames, LANES), 1)
    acc = jnp.zeros((frames, LANES), F32)
    for k in range(blocks):
        first, second, offset = split_run(starts[k], tiles)
        one = field[first & 1, pl.ds(first >> 1, frames, stride=planes * rows), :]
        two = field[second & 1, pl.ds(second >> 1, frames, stride=planes * rows), :]
        window = jnp.where(lane >= offset, one, two)
        voxel_windows[k] = window
        column = jnp.sum(window * compact[k : k + 1, :], axis=1, keepdims=True)
        acc = jnp.where(lane == k, column, acc)
    projected[...] = acc


def denoise_windows(starts, recording, pair, other, compact):
    frames, planes, rows, _ = recording.shape
    blocks = compact.shape[0]
    return pl.pallas_call(
        denoise_kernel,
        in_specs=[SMEM, VMEM, VMEM, VMEM, VMEM],
        out_specs=[VMEM, VMEM],
        out_shape=[
            pltpu.VMEM((blocks, frames, LANES), F32),
            pltpu.VMEM((frames, LANES), F32),
        ],
        scratch_shapes=[pltpu.VMEM((2, frames * planes * rows, LANES), F32)],
        compiler_params=PARAMS,
        name="denoise",
    )(near_scalar(starts), near(recording), near(pair), near(other), near(compact))


def as_column(line):
    count = line.shape[1]
    square = (count, count)
    same = iota(square, 0) == iota(square, 1)
    return jnp.sum(jnp.where(same, line, 0), axis=1, keepdims=True)


def combine_kernel(prior, owner, slot, projected, corr, piece, slot_prior):
    owners = prior.shape[0]
    blocks = corr.shape[0]
    frames = projected.shape[0]
    span = owners * SUBLANES
    flat = prior[...].astype(F32).reshape(span, LANES).astype(BF16)
    owner = as_column(owner[...])
    slot = as_column(slot[...])
    source = iota((blocks, span), 1)
    pick = jnp.concatenate(
        [onehot(source == owner * SUBLANES + i) for i in range(SUBLANES)], axis=0
    )
    found = jnp.dot(pick, flat, preferred_element_type=F32)
    lane = iota((blocks, LANES), 1)
    wanted = (lane >= LANES // 2) & (lane % blocks == slot)
    parts = [
        jnp.where(wanted, found[i * blocks : (i + 1) * blocks], 0.0).astype(BF16)
        for i in range(SUBLANES)
    ]
    wide = SUBLANES * LANES
    here = iota((wide, LANES), 0)
    frame_of = here // LANES + (here % LANES - LANES // 2) // blocks * SUBLANES
    frame_of = jnp.where(here % LANES >= LANES // 2, frame_of, -1)
    spread = onehot(frame_of == iota((wide, LANES), 1) % frames)
    earlier = jnp.dot(jnp.concatenate(parts, axis=1), spread, preferred_element_type=F32)
    slot_prior[...] = earlier
    repeat = jnp.where(
        iota((frames, LANES), 0) == iota((frames, LANES), 1) % frames, 1.0, 0.0
    )
    tiled = lax.dot_general(
        projected[...],
        repeat,
        (((0,), (0,)), ((), ())),
        precision=HIGHEST,
        preferred_element_type=F32,
    )[:blocks]
    value = tiled - jnp.dot(
        corr[:, :blocks], earlier, precision=HIGHEST, preferred_element_type=F32
    )
    row = iota((blocks, LANES), 0)
    value = jnp.where(lane // frames == row % SUBLANES, value, 0.0)
    lines = [
        jnp.sum(value[q * SUBLANES : (q + 1) * SUBLANES], axis=0, keepdims=True)
        for q in range(blocks // SUBLANES)
    ]
    terms = [two_terms(v) for v in lines]
    whole = jnp.concatenate([t[0] for t in terms] + [t[1] for t in terms], axis=0).astype(BF16)
    piece[...] = jnp.broadcast_to(whole[None], piece.shape)


def combine(prior, owner, slot, projected, corr):
    blocks = corr.shape[0]
    return pl.pallas_call(
        combine_kernel,
        in_specs=[VMEM] * 5,
        out_specs=[VMEM, VMEM],
        out_shape=[
            pltpu.VMEM(prior.shape, BF16),
            pltpu.VMEM((blocks, LANES), F32),
        ],
        compiler_params=PARAMS,
        name="combine",
    )(near(prior), near(owner), near(slot), near(projected), near(corr))


def update_kernel(
    prior, gathered, owner, slot, traces, slot_prior, voxel_windows, traces_new, sent
):
    owners = prior.shape[0]
    blocks = slot_prior.shape[0]
    frames, owned = traces.shape
    span = owners * SUBLANES
    flat = prior[...].astype(F32).reshape(span, LANES).astype(BF16)
    values = gathered[...].astype(F32).reshape(span, LANES).astype(BF16)
    lead = 4 * SUBLANES
    picks = onehot(iota((lead, LANES), 0) == iota((lead, LANES), 1))
    lists = lax.dot_general(
        picks, flat, (((1,), (1,)), ((), ())), preferred_element_type=F32
    )
    comps = lists[:SUBLANES] * float(owned) + lists[SUBLANES : 2 * SUBLANES]
    diags = lists[2 * SUBLANES : 3 * SUBLANES]
    position = lax.axis_index("bricks")
    asked = as_column(owner[...] * owned + slot[...])
    held = position * owned + iota((owned, 1), 0)
    target = jnp.concatenate([asked, held], axis=0).astype(F32)
    count = blocks + owned
    matches = []
    weight = jnp.zeros((count, span), F32)
    for j in range(SUBLANES):
        match = comps[j : j + 1] == target
        matches.append(onehot(match))
        weight = weight + jnp.where(match, diags[j : j + 1], 0.0)
    weight = jnp.sum(weight, axis=1, keepdims=True)
    sums = jnp.dot(jnp.concatenate(matches, axis=0), values, preferred_element_type=F32)
    group = iota((count, LANES), 1) // frames
    total = jnp.zeros((count, LANES), F32)
    for j in range(SUBLANES):
        total = jnp.where(group == j, sums[j * count : (j + 1) * count], total)
    shift = LANES // 2
    while shift >= frames:
        total = total + pltpu.roll(total, shift, 1)
        shift //= 2
    repeat = onehot(iota((frames, LANES), 0) == iota((frames, LANES), 1) % frames)
    mine = lax.dot_general(
        traces[...], repeat, (((0,), (0,)), ((), ())), preferred_element_type=F32
    )
    before = jnp.concatenate([slot_prior[...], mine], axis=0)
    after = jnp.maximum(0.0, before + total / (weight + 1.0))
    padded = jnp.concatenate([after, jnp.zeros((LANES - count, LANES), F32)], axis=0)
    turned = padded.T
    traces_new[...] = turned[:frames, blocks:count]
    slots = turned[:frames].astype(BF16).astype(F32)
    lane = iota((SUBLANES, LANES), 1)
    packed = jnp.where(
        lane < blocks,
        slots[:SUBLANES],
        jnp.where(lane < 2 * blocks, pltpu.roll(slots[SUBLANES:], blocks, 1), 0.0),
    )
    for k in range(blocks):
        line = jnp.sum(voxel_windows[k] * slots[:, k : k + 1], axis=0, keepdims=True)
        for g in range(sent.shape[0]):
            sent[g, k : k + 1, :] = line
    for g in range(sent.shape[0]):
        sent[g, blocks : blocks + SUBLANES, :] = packed


def update(prior, gathered, owner, slot, traces, slot_prior, voxel_windows, groups):
    blocks = slot_prior.shape[0]
    return pl.pallas_call(
        update_kernel,
        in_specs=[VMEM] * 7,
        out_specs=[VMEM, VMEM],
        out_shape=[
            pltpu.VMEM(traces.shape, F32),
            pltpu.VMEM((groups, blocks + SUBLANES, LANES), F32),
        ],
        compiler_params=PARAMS,
        name="update",
    )(
        near(prior),
        near(gathered),
        near(owner),
        near(slot),
        near(traces),
        near(slot_prior),
        near(voxel_windows),
    )


def finish_kernel(starts, shared, windows, compact, fresh, out, traces_new):
    traces_new[...] = fresh[...]
    blocks, voxels = out.shape
    tiles = voxels // LANES
    groups = shared.shape[0]
    lane = iota((blocks, LANES), 1)
    row = iota((blocks, LANES), 0)
    out[...] = jnp.zeros(out.shape, out.dtype)
    product = shared[0, :blocks, :]
    for g in range(1, groups):
        product = product + shared[g, :blocks, :]
    slots = jnp.concatenate([shared[g, blocks:, :] for g in range(groups)], axis=0).astype(BF16)
    both = lax.dot_general(slots, slots, (((0,), (0,)), ((), ())), preferred_element_type=F32)
    gram = both[:blocks] + pltpu.roll(both[blocks : 2 * blocks], LANES - blocks, 1)
    norm = jnp.sum(jnp.where(lane == row, gram, 0.0), axis=1, keepdims=True) + 1.0
    spread = jnp.concatenate(
        [
            jnp.sum(windows[k].astype(F32) * gram[:, k : k + 1], axis=0, keepdims=True)
            for k in range(blocks)
        ],
        axis=0,
    )
    current = compact[...]
    stepped = jnp.maximum(current + (product - spread) / norm, 0.0)
    stepped = jnp.where(current > 0, stepped, 0.0)
    for k in range(blocks):
        first, second, offset = split_run(starts[k], tiles)
        for index, part in ((first, lane >= offset), (second, lane < offset)):
            at = lane_tile(index)
            old = out[:, at].astype(F32)
            out[:, at] = jnp.where((row == k) & part, stepped, old).astype(out.dtype)


def finish(starts, shared, windows, compact, fresh, voxels):
    blocks = windows.shape[0]
    return pl.pallas_call(
        finish_kernel,
        in_specs=[SMEM, VMEM, VMEM, VMEM, VMEM],
        out_specs=[VMEM, VMEM],
        out_shape=[
            jax.ShapeDtypeStruct((blocks, voxels), BF16),
            jax.ShapeDtypeStruct(fresh.shape, fresh.dtype),
        ],
        compiler_params=PARAMS,
        name="finish",
    )(near_scalar(starts), near(shared), near(windows), near(compact), near(fresh))


def swapped(recording):
    count = lax.axis_size("bricks")
    across = [(i, i + 1) for i in range(1, count - 1, 2)]
    within = [(i, i + 1) for i in range(0, count, 2)]
    other = lax.ppermute(recording, "bricks", across + [(b, a) for a, b in across])
    pair = lax.ppermute(recording, "bricks", within + [(b, a) for a, b in within])
    return pair, other


def shards(recording, traces, footprints, block_owner, block_slot):
    voxels = footprints.shape[1]
    owners = lax.axis_size("bricks")
    groups = lax.axis_size("frames")
    pair, other = swapped(recording)
    owner = block_owner.T
    slot = block_slot[None, :]
    starts, windows, compact, corr, piece = prepare(owner, slot, traces, footprints, owners)
    prior = lax.all_to_all(piece, "bricks", 0, 0)
    voxel_windows, projected = denoise_windows(starts, recording, pair, other, compact)
    partials, slot_prior = combine(prior, owner, slot, projected, corr)
    gathered = lax.all_to_all(partials, "bricks", 0, 0)
    fresh, sent = update(prior, gathered, owner, slot, traces, slot_prior, voxel_windows, groups)
    shared = lax.all_to_all(sent, "frames", 0, 0)
    footprints_new, traces_new = finish(starts, shared, windows, compact, fresh, voxels)
    return (traces_new, footprints_new)


def solution(mesh):
    return jax.shard_map(
        shards,
        mesh=mesh,
        in_specs=(
            P("frames", "bricks", None, None),
            P("frames", "bricks"),
            P("bricks", None),
            P("bricks", None),
            P("bricks"),
        ),
        out_specs=(P("frames", "bricks"), P("bricks", None)),
        check_vma=False,
    )
```

```python
import jax
import jax.numpy as jnp
from jax import lax
from jax.experimental import pallas as pl
from jax.experimental.pallas import tpu as pltpu
from jax.sharding import PartitionSpec as P


TIME_STEP = 0.14
HIGHEST = lax.Precision.HIGHEST
LANES = 128
SUBLANES = 8
F32 = jnp.float32
BF16 = jnp.bfloat16
VMEM = pl.BlockSpec(memory_space=pltpu.VMEM)
SMEM = pl.BlockSpec(memory_space=pltpu.SMEM)
PARAMS = pltpu.CompilerParams(vmem_limit_bytes=16 * 2**20)


def near(array):
    return pltpu.with_memory_space_constraint(array, pltpu.VMEM)


def far(array):
    return pltpu.with_memory_space_constraint(array, pltpu.HBM)


def near_scalar(array):
    return pltpu.with_memory_space_constraint(array, pltpu.SMEM)


def iota(shape, axis):
    return lax.broadcasted_iota(jnp.int32, shape, axis)


def onehot(mask):
    return jnp.where(mask, 1.0, 0.0).astype(BF16)


def split_run(start, tiles):
    first = start >> 7
    return first, (first + 1) & (tiles - 1), start & (LANES - 1)


def lane_tile(index):
    return pl.ds(pl.multiple_of(index * LANES, LANES), LANES)


def two_terms(value):
    high = value.astype(BF16).astype(F32)
    return high, value - high


def as_column(line):
    count = line.shape[1]
    square = (count, count)
    same = iota(square, 0) == iota(square, 1)
    return jnp.sum(jnp.where(same, line, 0), axis=1, keepdims=True)


def label_rows(owner, slot, traces):
    frames, owned = traces.shape
    blocks = owner.shape[1]
    lane = iota((1, LANES), 1)
    gap = jnp.zeros((1, LANES - blocks), F32)
    lists = [jnp.concatenate([x[...].astype(F32), gap], axis=1) for x in (owner, slot)]
    rows = []
    for q in range(blocks // SUBLANES):
        first = pltpu.roll(lists[0], (LANES - q * SUBLANES) % LANES, 1)
        second = pltpu.roll(lists[1], (LANES + SUBLANES - q * SUBLANES) % LANES, 1)
        rows.append(
            jnp.where(lane < SUBLANES, first, jnp.where(lane < 2 * SUBLANES, second, 0.0))
        )
    wide = jnp.concatenate(
        [traces[...].astype(F32), jnp.zeros((frames, LANES - owned), F32)], axis=1
    )
    lane = iota((SUBLANES, LANES), 1)
    half = LANES // 2
    moved = jnp.where(
        lane < half + owned,
        pltpu.roll(wide[:SUBLANES], half, 1),
        pltpu.roll(wide[SUBLANES:], half + owned, 1),
    )
    return jnp.concatenate(rows + rows, axis=0) + jnp.where(lane < half, 0.0, moved)


def prepare_kernel(owner, slot, traces, foot, starts, windows, compact, corr, labels, piece):
    blocks, voxels = foot.shape
    tiles = voxels // LANES
    acc = jnp.zeros((blocks, LANES), BF16)
    for t in range(1, tiles):
        cell = foot[:, t * LANES : (t + 1) * LANES]
        acc = acc + jnp.where(cell > 0, jnp.asarray(t, BF16), jnp.asarray(0, BF16))
    tile_of = acc.astype(F32)
    lowest = jnp.min(tile_of, axis=1, keepdims=True)
    highest = jnp.max(tile_of, axis=1, keepdims=True)
    first_tile = jnp.where(highest - lowest > 1.5, highest, lowest)
    behind = jnp.sum(jnp.where(tile_of != first_tile, 1.0, 0.0), axis=1, keepdims=True)
    begin = (first_tile * LANES + behind).astype(jnp.int32)
    lane = iota((blocks, LANES), 1)
    row = iota((blocks, LANES), 0)
    sums = jnp.zeros((blocks, LANES), F32)
    for k in range(blocks):
        start = begin[k, 0]
        starts[k] = start
        first, second, offset = split_run(start, tiles)
        one = foot[:, lane_tile(first)].astype(F32)
        two = foot[:, lane_tile(second)].astype(F32)
        window = jnp.where(lane >= offset, one, two)
        windows[k] = window.astype(BF16)
        own = window[k : k + 1]
        compact[k : k + 1, :] = own
        sums = jnp.where(lane == k, jnp.sum(window * own, axis=1, keepdims=True), sums)
    corr[...] = sums
    labels[...] = jnp.where(lane == 0, as_column(owner[...]), as_column(slot[...]))
    diag = jnp.sum(jnp.where(lane == row, sums, 0.0), axis=1, keepdims=True)
    placed = jnp.where(lane == 2 * SUBLANES + row % SUBLANES, diag, 0.0)
    groups = blocks // SUBLANES
    rows = [
        jnp.sum(placed[q * SUBLANES : (q + 1) * SUBLANES], axis=0, keepdims=True)
        for q in range(groups)
    ]
    terms = [two_terms(r) for r in rows]
    part = jnp.concatenate([t[0] for t in terms] + [t[1] for t in terms], axis=0)
    whole = (label_rows(owner, slot, traces) + part).astype(BF16)
    piece[...] = jnp.broadcast_to(whole[None], piece.shape)


def prepare(owner, slot, traces, footprints, owners):
    blocks, _ = footprints.shape
    return pl.pallas_call(
        prepare_kernel,
        in_specs=[VMEM] * 4,
        out_specs=[SMEM, VMEM, VMEM, VMEM, VMEM, VMEM],
        out_shape=[
            pltpu.SMEM((blocks,), jnp.int32),
            pltpu.VMEM((blocks, blocks, LANES), BF16),
            pltpu.VMEM((blocks, LANES), F32),
            pltpu.VMEM((blocks, LANES), F32),
            pltpu.VMEM((blocks, LANES), jnp.int32),
            pltpu.VMEM((owners, SUBLANES, LANES), BF16),
        ],
        compiler_params=PARAMS,
        name="prepare",
    )(far(owner), far(slot), far(traces), far(footprints))


def flux_of(difference):
    return difference / (1.0 + difference * difference)


def relax(planes, masks):
    first_row, last_row, first_col, last_col = masks
    across = [
        [[flux_of(planes[i + 1][z][y] - planes[i][z][y]) for y in range(2)] for z in range(2)]
        for i in range(len(planes) - 1)
    ]
    out = []
    for i in range(1, len(planes) - 1):
        u = planes[i]
        edge = [[flux_of(u[0][0]), flux_of(u[0][1])], [flux_of(u[1][0]), None]]
        total = [[across[i][z][y] - across[i - 1][z][y] for y in range(2)] for z in range(2)]
        for y in range(2):
            low = pltpu.roll(u[0][y], SUBLANES - 1, 0)
            high = pltpu.roll(u[1][y], SUBLANES - 1, 0)
            down_low = flux_of(jnp.where(last_row, high, low) - u[0][y])
            down_high = flux_of(jnp.where(last_row, 0.0, high) - u[1][y])
            up_low = pltpu.roll(down_low, 1, 0)
            up_high = pltpu.roll(down_high, 1, 0)
            total[0][y] = total[0][y] + (down_low - jnp.where(first_row, edge[0][y], up_low))
            total[1][y] = total[1][y] + (down_high - jnp.where(first_row, up_low, up_high))
        for z in range(2):
            low = pltpu.roll(u[z][0], LANES - 1, 1)
            high = pltpu.roll(u[z][1], LANES - 1, 1)
            right_low = flux_of(jnp.where(last_col, high, low) - u[z][0])
            right_high = flux_of(jnp.where(last_col, 0.0, high) - u[z][1])
            left_low = pltpu.roll(right_low, 1, 1)
            left_high = pltpu.roll(right_high, 1, 1)
            total[z][0] = total[z][0] + (right_low - jnp.where(first_col, edge[z][0], left_low))
            total[z][1] = total[z][1] + (right_high - jnp.where(first_col, left_low, left_high))
        out.append([[u[z][y] + TIME_STEP * total[z][y] for y in range(2)] for z in range(2)])
    return out


def quarters(plane):
    wide = plane.astype(F32)
    return [
        [wide[z * SUBLANES : (z + 1) * SUBLANES, y * LANES : (y + 1) * LANES] for y in range(2)]
        for z in range(2)
    ]


def scaled(plane, keep):
    return [[cell * keep for cell in line] for line in plane]


def denoise_kernel(starts, rec, pair, other, compact, voxel_windows, projected, field):
    frames, planes, rows, _ = rec.shape
    width = 3
    position = lax.axis_index("bricks")
    low_keep = jnp.where(position > 0, 1.0, 0.0)
    high_keep = jnp.where(position < lax.axis_size("bricks") - 1, 1.0, 0.0)
    row = iota((SUBLANES, LANES), 0)
    col = iota((SUBLANES, LANES), 1)
    masks = (row == 0, row == SUBLANES - 1, col == 0, col == LANES - 1)

    def one_frame(f, low, high):
        u = [quarters(low[f, planes - width + i]) for i in range(width)]
        u = u + [quarters(rec[f, i]) for i in range(planes)]
        u = u + [quarters(high[f, i]) for i in range(width)]
        for sweep in range(width):
            u = relax(u, masks)
            extra = width - 1 - sweep
            if extra:
                u = (
                    [scaled(v, low_keep) for v in u[:extra]]
                    + u[extra : extra + planes]
                    + [scaled(v, high_keep) for v in u[extra + planes :]]
                )
        for i in range(planes):
            for z in range(2):
                for y in range(2):
                    at = pl.ds((i * rows + z * SUBLANES) * frames + f, SUBLANES, stride=frames)
                    field[y, at, :] = u[i][z][y].astype(BF16).astype(F32)

    odd = position % 2 == 1
    for is_odd, low, high in ((True, pair, other), (False, other, pair)):

        @pl.when(odd if is_odd else jnp.logical_not(odd))
        def _(low=low, high=high):
            pl.loop(0, frames)(lambda f: one_frame(f, low, high))

    blocks = compact.shape[0]
    tiles = planes * rows * 2
    lane = iota((frames, LANES), 1)
    acc = jnp.zeros((frames, LANES), F32)
    for k in range(blocks):
        first, second, offset = split_run(starts[k], tiles)
        one = field[first & 1, pl.ds(pl.multiple_of((first >> 1) * frames, frames), frames), :]
        two = field[second & 1, pl.ds(pl.multiple_of((second >> 1) * frames, frames), frames), :]
        window = jnp.where(lane >= offset, one, two)
        voxel_windows[k] = window
        column = jnp.sum(window * compact[k : k + 1, :], axis=1, keepdims=True)
        acc = jnp.where(lane == k, column, acc)
    projected[...] = acc


def denoise_windows(starts, recording, pair, other, compact):
    frames, planes, rows, _ = recording.shape
    blocks = compact.shape[0]
    return pl.pallas_call(
        denoise_kernel,
        in_specs=[SMEM, VMEM, VMEM, VMEM, VMEM],
        out_specs=[VMEM, VMEM],
        out_shape=[
            pltpu.VMEM((blocks, frames, LANES), F32),
            pltpu.VMEM((frames, LANES), F32),
        ],
        scratch_shapes=[pltpu.VMEM((2, frames * planes * rows, LANES), F32)],
        compiler_params=PARAMS,
        name="denoise",
    )(near_scalar(starts), near(recording), near(pair), near(other), near(compact))


def combine_kernel(prior, labels, projected, corr, piece, slot_prior):
    owners = prior.shape[0]
    blocks = corr.shape[0]
    frames = projected.shape[0]
    span = owners * SUBLANES
    flat = prior[...].astype(F32).reshape(span, LANES).astype(BF16)
    owner = labels[:, 0:1]
    slot = labels[:, 1:2]
    source = iota((blocks, span), 1)
    pick = jnp.concatenate(
        [onehot(source == owner * SUBLANES + i) for i in range(SUBLANES)], axis=0
    )
    found = jnp.dot(pick, flat, preferred_element_type=F32)
    lane = iota((blocks, LANES), 1)
    wanted = (lane >= LANES // 2) & (lane % blocks == slot)
    parts = [
        jnp.where(wanted, found[i * blocks : (i + 1) * blocks], 0.0).astype(BF16)
        for i in range(SUBLANES)
    ]
    wide = SUBLANES * LANES
    here = iota((wide, LANES), 0)
    frame_of = here // LANES + (here % LANES - LANES // 2) // blocks * SUBLANES
    frame_of = jnp.where(here % LANES >= LANES // 2, frame_of, -1)
    spread = onehot(frame_of == iota((wide, LANES), 1) % frames)
    earlier = jnp.dot(jnp.concatenate(parts, axis=1), spread, preferred_element_type=F32)
    slot_prior[...] = earlier
    repeat = jnp.where(
        iota((frames, LANES), 0) == iota((frames, LANES), 1) % frames, 1.0, 0.0
    )
    tiled = lax.dot_general(
        projected[...],
        repeat,
        (((0,), (0,)), ((), ())),
        precision=HIGHEST,
        preferred_element_type=F32,
    )[:blocks]
    value = tiled - jnp.dot(
        corr[:, :blocks], earlier, precision=HIGHEST, preferred_element_type=F32
    )
    row = iota((blocks, LANES), 0)
    value = jnp.where(lane // frames == row % SUBLANES, value, 0.0)
    lines = [
        jnp.sum(value[q * SUBLANES : (q + 1) * SUBLANES], axis=0, keepdims=True)
        for q in range(blocks // SUBLANES)
    ]
    terms = [two_terms(v) for v in lines]
    whole = jnp.concatenate([t[0] for t in terms] + [t[1] for t in terms], axis=0).astype(BF16)
    piece[...] = jnp.broadcast_to(whole[None], piece.shape)


def combine(prior, labels, projected, corr):
    blocks = corr.shape[0]
    return pl.pallas_call(
        combine_kernel,
        in_specs=[VMEM] * 4,
        out_specs=[VMEM, VMEM],
        out_shape=[
            pltpu.VMEM(prior.shape, BF16),
            pltpu.VMEM((blocks, LANES), F32),
        ],
        compiler_params=PARAMS,
        name="combine",
    )(near(prior), near(labels), near(projected), near(corr))


def update_kernel(
    prior, gathered, labels, traces, slot_prior, voxel_windows, traces_new, sent
):
    owners = prior.shape[0]
    blocks = slot_prior.shape[0]
    frames, owned = traces.shape
    span = owners * SUBLANES
    flat = prior[...].astype(F32).reshape(span, LANES).astype(BF16)
    values = gathered[...].astype(F32).reshape(span, LANES).astype(BF16)
    lead = 4 * SUBLANES
    picks = onehot(iota((lead, LANES), 0) == iota((lead, LANES), 1))
    lists = lax.dot_general(
        picks, flat, (((1,), (1,)), ((), ())), preferred_element_type=F32
    )
    comps = lists[:SUBLANES] * float(owned) + lists[SUBLANES : 2 * SUBLANES]
    diags = lists[2 * SUBLANES : 3 * SUBLANES]
    position = lax.axis_index("bricks")
    asked = labels[:, 0:1] * owned + labels[:, 1:2]
    held = position * owned + iota((owned, 1), 0)
    target = jnp.concatenate([asked, held], axis=0).astype(F32)
    count = blocks + owned
    matches = []
    weight = jnp.zeros((count, span), F32)
    for j in range(SUBLANES):
        match = comps[j : j + 1] == target
        matches.append(onehot(match))
        weight = weight + jnp.where(match, diags[j : j + 1], 0.0)
    weight = jnp.sum(weight, axis=1, keepdims=True)
    sums = jnp.dot(jnp.concatenate(matches, axis=0), values, preferred_element_type=F32)
    group = iota((count, LANES), 1) // frames
    total = jnp.zeros((count, LANES), F32)
    for j in range(SUBLANES):
        total = jnp.where(group == j, sums[j * count : (j + 1) * count], total)
    shift = LANES // 2
    while shift >= frames:
        total = total + pltpu.roll(total, shift, 1)
        shift //= 2
    repeat = onehot(iota((frames, LANES), 0) == iota((frames, LANES), 1) % frames)
    mine = lax.dot_general(
        traces[...], repeat, (((0,), (0,)), ((), ())), preferred_element_type=F32
    )
    before = jnp.concatenate([slot_prior[...], mine], axis=0)
    after = jnp.maximum(0.0, before + total / (weight + 1.0))
    padded = jnp.concatenate([after, jnp.zeros((LANES - count, LANES), F32)], axis=0)
    turned = padded.T
    traces_new[...] = turned[:frames, blocks:count]
    slots = turned[:frames].astype(BF16).astype(F32)
    lane = iota((SUBLANES, LANES), 1)
    packed = jnp.where(
        lane < blocks,
        slots[:SUBLANES],
        jnp.where(lane < 2 * blocks, pltpu.roll(slots[SUBLANES:], blocks, 1), 0.0),
    )
    for k in range(blocks):
        line = jnp.sum(voxel_windows[k] * slots[:, k : k + 1], axis=0, keepdims=True)
        for g in range(sent.shape[0]):
            sent[g, k : k + 1, :] = line
    for g in range(sent.shape[0]):
        sent[g, blocks : blocks + SUBLANES, :] = packed


def update(prior, gathered, labels, traces, slot_prior, voxel_windows, groups):
    blocks = slot_prior.shape[0]
    return pl.pallas_call(
        update_kernel,
        in_specs=[VMEM] * 6,
        out_specs=[VMEM, VMEM],
        out_shape=[
            pltpu.VMEM(traces.shape, F32),
            pltpu.VMEM((groups, blocks + SUBLANES, LANES), F32),
        ],
        compiler_params=PARAMS,
        name="update",
    )(
        near(prior),
        near(gathered),
        near(labels),
        near(traces),
        near(slot_prior),
        near(voxel_windows),
    )


def finish_kernel(starts, shared, windows, compact, fresh, out, traces_new):
    traces_new[...] = fresh[...]
    blocks, voxels = out.shape
    tiles = voxels // LANES
    groups = shared.shape[0]
    lane = iota((blocks, LANES), 1)
    row = iota((blocks, LANES), 0)
    out[...] = jnp.zeros(out.shape, out.dtype)
    product = shared[0, :blocks, :]
    for g in range(1, groups):
        product = product + shared[g, :blocks, :]
    slots = jnp.concatenate([shared[g, blocks:, :] for g in range(groups)], axis=0).astype(BF16)
    both = lax.dot_general(slots, slots, (((0,), (0,)), ((), ())), preferred_element_type=F32)
    gram = both[:blocks] + pltpu.roll(both[blocks : 2 * blocks], LANES - blocks, 1)
    norm = jnp.sum(jnp.where(lane == row, gram, 0.0), axis=1, keepdims=True) + 1.0
    spread = jnp.concatenate(
        [
            jnp.sum(windows[k].astype(F32) * gram[:, k : k + 1], axis=0, keepdims=True)
            for k in range(blocks)
        ],
        axis=0,
    )
    current = compact[...]
    stepped = jnp.maximum(current + (product - spread) / norm, 0.0)
    stepped = jnp.where(current > 0, stepped, 0.0)
    for k in range(blocks):
        first, second, offset = split_run(starts[k], tiles)
        for index, part in ((first, lane >= offset), (second, lane < offset)):
            at = lane_tile(index)
            old = out[:, at].astype(F32)
            out[:, at] = jnp.where((row == k) & part, stepped, old).astype(out.dtype)


def finish(starts, shared, windows, compact, fresh, voxels):
    blocks = windows.shape[0]
    return pl.pallas_call(
        finish_kernel,
        in_specs=[SMEM, VMEM, VMEM, VMEM, VMEM],
        out_specs=[VMEM, VMEM],
        out_shape=[
            jax.ShapeDtypeStruct((blocks, voxels), BF16),
            jax.ShapeDtypeStruct(fresh.shape, fresh.dtype),
        ],
        compiler_params=PARAMS,
        name="finish",
    )(near_scalar(starts), near(shared), near(windows), near(compact), near(fresh))


def swapped(recording):
    count = lax.axis_size("bricks")
    across = [(i, i + 1) for i in range(1, count - 1, 2)]
    within = [(i, i + 1) for i in range(0, count, 2)]
    other = lax.ppermute(recording, "bricks", across + [(b, a) for a, b in across])
    pair = lax.ppermute(recording, "bricks", within + [(b, a) for a, b in within])
    return pair, other


def shards(recording, traces, footprints, block_owner, block_slot):
    voxels = footprints.shape[1]
    owners = lax.axis_size("bricks")
    groups = lax.axis_size("frames")
    pair, other = swapped(recording)
    owner = block_owner.T
    slot = block_slot[None, :]
    starts, windows, compact, corr, labels, piece = prepare(owner, slot, traces, footprints, owners)
    prior = lax.all_to_all(piece, "bricks", 0, 0)
    voxel_windows, projected = denoise_windows(starts, recording, pair, other, compact)
    partials, slot_prior = combine(prior, labels, projected, corr)
    gathered = lax.all_to_all(partials, "bricks", 0, 0)
    fresh, sent = update(
        prior, gathered, labels, traces, slot_prior, voxel_windows, groups
    )
    shared = lax.all_to_all(sent, "frames", 0, 0)
    footprints_new, traces_new = finish(starts, shared, windows, compact, fresh, voxels)
    return (traces_new, footprints_new)


def solution(mesh):
    return jax.shard_map(
        shards,
        mesh=mesh,
        in_specs=(
            P("frames", "bricks", None, None),
            P("frames", "bricks"),
            P("bricks", None),
            P("bricks", None),
            P("bricks"),
        ),
        out_specs=(P("frames", "bricks"), P("bricks", None)),
        check_vma=False,
    )
```

```python
import jax
import jax.numpy as jnp
from jax import lax
from jax.experimental import pallas as pl
from jax.experimental.pallas import tpu as pltpu
from jax.sharding import PartitionSpec as P


TIME_STEP = 0.14
HIGHEST = lax.Precision.HIGHEST
LANES = 128
SUBLANES = 8
F32 = jnp.float32
MARK_SCALE = 16384.0
BF16 = jnp.bfloat16
VMEM = pl.BlockSpec(memory_space=pltpu.VMEM)
SMEM = pl.BlockSpec(memory_space=pltpu.SMEM)
PARAMS = pltpu.CompilerParams(vmem_limit_bytes=16 * 2**20)


def near(array):
    return pltpu.with_memory_space_constraint(array, pltpu.VMEM)


def far(array):
    return pltpu.with_memory_space_constraint(array, pltpu.HBM)


def near_scalar(array):
    return pltpu.with_memory_space_constraint(array, pltpu.SMEM)


def iota(shape, axis):
    return lax.broadcasted_iota(jnp.int32, shape, axis)


def onehot(mask):
    return jnp.where(mask, 1.0, 0.0).astype(BF16)


def split_run(start, tiles):
    first = start >> 7
    return first, (first + 1) & (tiles - 1), start & (LANES - 1)


def lane_tile(index):
    return pl.ds(pl.multiple_of(index * LANES, LANES), LANES)


def two_terms(value):
    high = value.astype(BF16).astype(F32)
    return high, value - high


def as_column(line):
    count = line.shape[1]
    square = (count, count)
    same = iota(square, 0) == iota(square, 1)
    return jnp.sum(jnp.where(same, line, 0), axis=1, keepdims=True)


def label_rows(owner, slot, traces):
    frames, owned = traces.shape
    blocks = owner.shape[1]
    lane = iota((1, LANES), 1)
    gap = jnp.zeros((1, LANES - blocks), F32)
    lists = [jnp.concatenate([x[...].astype(F32), gap], axis=1) for x in (owner, slot)]
    rows = []
    for q in range(blocks // SUBLANES):
        first = pltpu.roll(lists[0], (LANES - q * SUBLANES) % LANES, 1)
        second = pltpu.roll(lists[1], (LANES + SUBLANES - q * SUBLANES) % LANES, 1)
        rows.append(
            jnp.where(lane < SUBLANES, first, jnp.where(lane < 2 * SUBLANES, second, 0.0))
        )
    wide = jnp.concatenate(
        [traces[...].astype(F32), jnp.zeros((frames, LANES - owned), F32)], axis=1
    )
    lane = iota((SUBLANES, LANES), 1)
    half = LANES // 2
    moved = jnp.where(
        lane < half + owned,
        pltpu.roll(wide[:SUBLANES], half, 1),
        pltpu.roll(wide[SUBLANES:], half + owned, 1),
    )
    return jnp.concatenate(rows + rows, axis=0) + jnp.where(lane < half, 0.0, moved)


def prepare_kernel(owner, slot, traces, foot, starts, windows, compact, corr, labels, piece):
    blocks, voxels = foot.shape
    tiles = voxels // LANES
    acc = jnp.zeros((blocks, LANES), BF16)
    for t in range(1, tiles):
        cell = foot[:, t * LANES : (t + 1) * LANES]
        acc = jnp.maximum(acc, jnp.minimum(cell, jnp.asarray(t / MARK_SCALE, BF16)))
    tile_of = acc.astype(F32) * MARK_SCALE
    lowest = jnp.min(tile_of, axis=1, keepdims=True)
    highest = jnp.max(tile_of, axis=1, keepdims=True)
    first_tile = jnp.where(highest - lowest > 1.5, highest, lowest)
    behind = jnp.sum(jnp.where(tile_of != first_tile, 1.0, 0.0), axis=1, keepdims=True)
    begin = (first_tile * LANES + behind).astype(jnp.int32)
    lane = iota((blocks, LANES), 1)
    row = iota((blocks, LANES), 0)
    sums = jnp.zeros((blocks, LANES), F32)
    for k in range(blocks):
        start = begin[k, 0]
        starts[k] = start
        first, second, offset = split_run(start, tiles)
        one = foot[:, lane_tile(first)].astype(F32)
        two = foot[:, lane_tile(second)].astype(F32)
        window = jnp.where(lane >= offset, one, two)
        windows[k] = window.astype(BF16)
        own = window[k : k + 1]
        compact[k : k + 1, :] = own
        sums = jnp.where(lane == k, jnp.sum(window * own, axis=1, keepdims=True), sums)
    corr[...] = sums
    labels[...] = jnp.where(lane == 0, as_column(owner[...]), as_column(slot[...]))
    diag = jnp.sum(jnp.where(lane == row, sums, 0.0), axis=1, keepdims=True)
    placed = jnp.where(lane == 2 * SUBLANES + row % SUBLANES, diag, 0.0)
    groups = blocks // SUBLANES
    rows = [
        jnp.sum(placed[q * SUBLANES : (q + 1) * SUBLANES], axis=0, keepdims=True)
        for q in range(groups)
    ]
    terms = [two_terms(r) for r in rows]
    part = jnp.concatenate([t[0] for t in terms] + [t[1] for t in terms], axis=0)
    whole = (label_rows(owner, slot, traces) + part).astype(BF16)
    piece[...] = jnp.broadcast_to(whole[None], piece.shape)


def prepare(owner, slot, traces, footprints, owners):
    blocks, _ = footprints.shape
    return pl.pallas_call(
        prepare_kernel,
        in_specs=[VMEM] * 4,
        out_specs=[SMEM, VMEM, VMEM, VMEM, VMEM, VMEM],
        out_shape=[
            pltpu.SMEM((blocks,), jnp.int32),
            pltpu.VMEM((blocks, blocks, LANES), BF16),
            pltpu.VMEM((blocks, LANES), F32),
            pltpu.VMEM((blocks, LANES), F32),
            pltpu.VMEM((blocks, LANES), jnp.int32),
            pltpu.VMEM((owners, SUBLANES, LANES), BF16),
        ],
        compiler_params=PARAMS,
        name="prepare",
    )(far(owner), far(slot), far(traces), far(footprints))


def flux_of(difference):
    return difference / (1.0 + difference * difference)


def relax(planes, masks):
    first_row, last_row, first_col, last_col = masks
    across = [
        [[flux_of(planes[i + 1][z][y] - planes[i][z][y]) for y in range(2)] for z in range(2)]
        for i in range(len(planes) - 1)
    ]
    out = []
    for i in range(1, len(planes) - 1):
        u = planes[i]
        edge = [[flux_of(u[0][0]), flux_of(u[0][1])], [flux_of(u[1][0]), None]]
        total = [[across[i][z][y] - across[i - 1][z][y] for y in range(2)] for z in range(2)]
        for y in range(2):
            low = pltpu.roll(u[0][y], SUBLANES - 1, 0)
            high = pltpu.roll(u[1][y], SUBLANES - 1, 0)
            down_low = flux_of(jnp.where(last_row, high, low) - u[0][y])
            down_high = flux_of(jnp.where(last_row, 0.0, high) - u[1][y])
            up_low = pltpu.roll(down_low, 1, 0)
            up_high = pltpu.roll(down_high, 1, 0)
            total[0][y] = total[0][y] + (down_low - jnp.where(first_row, edge[0][y], up_low))
            total[1][y] = total[1][y] + (down_high - jnp.where(first_row, up_low, up_high))
        for z in range(2):
            low = pltpu.roll(u[z][0], LANES - 1, 1)
            high = pltpu.roll(u[z][1], LANES - 1, 1)
            right_low = flux_of(jnp.where(last_col, high, low) - u[z][0])
            right_high = flux_of(jnp.where(last_col, 0.0, high) - u[z][1])
            left_low = pltpu.roll(right_low, 1, 1)
            left_high = pltpu.roll(right_high, 1, 1)
            total[z][0] = total[z][0] + (right_low - jnp.where(first_col, edge[z][0], left_low))
            total[z][1] = total[z][1] + (right_high - jnp.where(first_col, left_low, left_high))
        out.append([[u[z][y] + TIME_STEP * total[z][y] for y in range(2)] for z in range(2)])
    return out


def quarters(plane):
    wide = plane.astype(F32)
    return [
        [wide[z * SUBLANES : (z + 1) * SUBLANES, y * LANES : (y + 1) * LANES] for y in range(2)]
        for z in range(2)
    ]


def scaled(plane, keep):
    return [[cell * keep for cell in line] for line in plane]


def denoise_kernel(starts, rec, pair, other, compact, voxel_windows, projected, field):
    frames, planes, rows, _ = rec.shape
    width = 3
    position = lax.axis_index("bricks")
    low_keep = jnp.where(position > 0, 1.0, 0.0)
    high_keep = jnp.where(position < lax.axis_size("bricks") - 1, 1.0, 0.0)
    row = iota((SUBLANES, LANES), 0)
    col = iota((SUBLANES, LANES), 1)
    masks = (row == 0, row == SUBLANES - 1, col == 0, col == LANES - 1)

    def one_frame(f, low, high):
        u = [quarters(low[f, planes - width + i]) for i in range(width)]
        u = u + [quarters(rec[f, i]) for i in range(planes)]
        u = u + [quarters(high[f, i]) for i in range(width)]
        for sweep in range(width):
            u = relax(u, masks)
            extra = width - 1 - sweep
            if extra:
                u = (
                    [scaled(v, low_keep) for v in u[:extra]]
                    + u[extra : extra + planes]
                    + [scaled(v, high_keep) for v in u[extra + planes :]]
                )
        for i in range(planes):
            for z in range(2):
                for y in range(2):
                    at = pl.ds((i * rows + z * SUBLANES) * frames + f, SUBLANES, stride=frames)
                    field[y, at, :] = u[i][z][y].astype(BF16).astype(F32)

    odd = position % 2 == 1
    for is_odd, low, high in ((True, pair, other), (False, other, pair)):

        @pl.when(odd if is_odd else jnp.logical_not(odd))
        def _(low=low, high=high):
            pl.loop(0, frames)(lambda f: one_frame(f, low, high))

    blocks = compact.shape[0]
    tiles = planes * rows * 2
    lane = iota((frames, LANES), 1)
    acc = jnp.zeros((frames, LANES), F32)
    for k in range(blocks):
        first, second, offset = split_run(starts[k], tiles)
        one = field[first & 1, pl.ds(pl.multiple_of((first >> 1) * frames, frames), frames), :]
        two = field[second & 1, pl.ds(pl.multiple_of((second >> 1) * frames, frames), frames), :]
        window = jnp.where(lane >= offset, one, two)
        voxel_windows[k] = window
        column = jnp.sum(window * compact[k : k + 1, :], axis=1, keepdims=True)
        acc = jnp.where(lane == k, column, acc)
    projected[...] = acc


def denoise_windows(starts, recording, pair, other, compact):
    frames, planes, rows, _ = recording.shape
    blocks = compact.shape[0]
    return pl.pallas_call(
        denoise_kernel,
        in_specs=[SMEM, VMEM, VMEM, VMEM, VMEM],
        out_specs=[VMEM, VMEM],
        out_shape=[
            pltpu.VMEM((blocks, frames, LANES), F32),
            pltpu.VMEM((frames, LANES), F32),
        ],
        scratch_shapes=[pltpu.VMEM((2, frames * planes * rows, LANES), F32)],
        compiler_params=PARAMS,
        name="denoise",
    )(near_scalar(starts), near(recording), near(pair), near(other), near(compact))


def combine_kernel(prior, labels, projected, corr, piece, slot_prior):
    owners = prior.shape[0]
    blocks = corr.shape[0]
    frames = projected.shape[0]
    span = owners * SUBLANES
    flat = prior[...].astype(F32).reshape(span, LANES).astype(BF16)
    owner = labels[:, 0:1]
    slot = labels[:, 1:2]
    source = iota((blocks, span), 1)
    pick = jnp.concatenate(
        [onehot(source == owner * SUBLANES + i) for i in range(SUBLANES)], axis=0
    )
    found = jnp.dot(pick, flat, preferred_element_type=F32)
    lane = iota((blocks, LANES), 1)
    wanted = (lane >= LANES // 2) & (lane % blocks == slot)
    parts = [
        jnp.where(wanted, found[i * blocks : (i + 1) * blocks], 0.0).astype(BF16)
        for i in range(SUBLANES)
    ]
    wide = SUBLANES * LANES
    here = iota((wide, LANES), 0)
    frame_of = here // LANES + (here % LANES - LANES // 2) // blocks * SUBLANES
    frame_of = jnp.where(here % LANES >= LANES // 2, frame_of, -1)
    spread = onehot(frame_of == iota((wide, LANES), 1) % frames)
    earlier = jnp.dot(jnp.concatenate(parts, axis=1), spread, preferred_element_type=F32)
    slot_prior[...] = earlier
    repeat = jnp.where(
        iota((frames, LANES), 0) == iota((frames, LANES), 1) % frames, 1.0, 0.0
    )
    tiled = lax.dot_general(
        projected[...],
        repeat,
        (((0,), (0,)), ((), ())),
        precision=HIGHEST,
        preferred_element_type=F32,
    )[:blocks]
    value = tiled - jnp.dot(
        corr[:, :blocks], earlier, precision=HIGHEST, preferred_element_type=F32
    )
    row = iota((blocks, LANES), 0)
    value = jnp.where(lane // frames == row % SUBLANES, value, 0.0)
    lines = [
        jnp.sum(value[q * SUBLANES : (q + 1) * SUBLANES], axis=0, keepdims=True)
        for q in range(blocks // SUBLANES)
    ]
    terms = [two_terms(v) for v in lines]
    whole = jnp.concatenate([t[0] for t in terms] + [t[1] for t in terms], axis=0).astype(BF16)
    piece[...] = jnp.broadcast_to(whole[None], piece.shape)


def combine(prior, labels, projected, corr):
    blocks = corr.shape[0]
    return pl.pallas_call(
        combine_kernel,
        in_specs=[VMEM] * 4,
        out_specs=[VMEM, VMEM],
        out_shape=[
            pltpu.VMEM(prior.shape, BF16),
            pltpu.VMEM((blocks, LANES), F32),
        ],
        compiler_params=PARAMS,
        name="combine",
    )(near(prior), near(labels), near(projected), near(corr))


def update_kernel(
    prior, gathered, labels, traces, slot_prior, voxel_windows, traces_new, sent
):
    owners = prior.shape[0]
    blocks = slot_prior.shape[0]
    frames, owned = traces.shape
    span = owners * SUBLANES
    flat = prior[...].astype(F32).reshape(span, LANES).astype(BF16)
    values = gathered[...].astype(F32).reshape(span, LANES).astype(BF16)
    lead = 4 * SUBLANES
    picks = onehot(iota((lead, LANES), 0) == iota((lead, LANES), 1))
    lists = lax.dot_general(
        picks, flat, (((1,), (1,)), ((), ())), preferred_element_type=F32
    )
    comps = lists[:SUBLANES] * float(owned) + lists[SUBLANES : 2 * SUBLANES]
    diags = lists[2 * SUBLANES : 3 * SUBLANES]
    position = lax.axis_index("bricks")
    asked = labels[:, 0:1] * owned + labels[:, 1:2]
    held = position * owned + iota((owned, 1), 0)
    target = jnp.concatenate([asked, held], axis=0).astype(F32)
    count = blocks + owned
    matches = []
    weight = jnp.zeros((count, span), F32)
    for j in range(SUBLANES):
        match = comps[j : j + 1] == target
        matches.append(onehot(match))
        weight = weight + jnp.where(match, diags[j : j + 1], 0.0)
    weight = jnp.sum(weight, axis=1, keepdims=True)
    sums = jnp.dot(jnp.concatenate(matches, axis=0), values, preferred_element_type=F32)
    group = iota((count, LANES), 1) // frames
    total = jnp.zeros((count, LANES), F32)
    for j in range(SUBLANES):
        total = jnp.where(group == j, sums[j * count : (j + 1) * count], total)
    shift = LANES // 2
    while shift >= frames:
        total = total + pltpu.roll(total, shift, 1)
        shift //= 2
    repeat = onehot(iota((frames, LANES), 0) == iota((frames, LANES), 1) % frames)
    mine = lax.dot_general(
        traces[...], repeat, (((0,), (0,)), ((), ())), preferred_element_type=F32
    )
    before = jnp.concatenate([slot_prior[...], mine], axis=0)
    after = jnp.maximum(0.0, before + total / (weight + 1.0))
    padded = jnp.concatenate([after, jnp.zeros((LANES - count, LANES), F32)], axis=0)
    turned = padded.T
    traces_new[...] = turned[:frames, blocks:count]
    slots = turned[:frames].astype(BF16).astype(F32)
    lane = iota((SUBLANES, LANES), 1)
    packed = jnp.where(
        lane < blocks,
        slots[:SUBLANES],
        jnp.where(lane < 2 * blocks, pltpu.roll(slots[SUBLANES:], blocks, 1), 0.0),
    )
    for k in range(blocks):
        line = jnp.sum(voxel_windows[k] * slots[:, k : k + 1], axis=0, keepdims=True)
        for g in range(sent.shape[0]):
            sent[g, k : k + 1, :] = line
    for g in range(sent.shape[0]):
        sent[g, blocks : blocks + SUBLANES, :] = packed


def update(prior, gathered, labels, traces, slot_prior, voxel_windows, groups):
    blocks = slot_prior.shape[0]
    return pl.pallas_call(
        update_kernel,
        in_specs=[VMEM] * 6,
        out_specs=[VMEM, VMEM],
        out_shape=[
            pltpu.VMEM(traces.shape, F32),
            pltpu.VMEM((groups, blocks + SUBLANES, LANES), F32),
        ],
        compiler_params=PARAMS,
        name="update",
    )(
        near(prior),
        near(gathered),
        near(labels),
        near(traces),
        near(slot_prior),
        near(voxel_windows),
    )


def finish_kernel(starts, shared, windows, compact, fresh, out, traces_new):
    traces_new[...] = fresh[...]
    blocks, voxels = out.shape
    tiles = voxels // LANES
    groups = shared.shape[0]
    lane = iota((blocks, LANES), 1)
    row = iota((blocks, LANES), 0)
    out[...] = jnp.zeros(out.shape, out.dtype)
    product = shared[0, :blocks, :]
    for g in range(1, groups):
        product = product + shared[g, :blocks, :]
    slots = jnp.concatenate([shared[g, blocks:, :] for g in range(groups)], axis=0).astype(BF16)
    both = lax.dot_general(slots, slots, (((0,), (0,)), ((), ())), preferred_element_type=F32)
    gram = both[:blocks] + pltpu.roll(both[blocks : 2 * blocks], LANES - blocks, 1)
    norm = jnp.sum(jnp.where(lane == row, gram, 0.0), axis=1, keepdims=True) + 1.0
    spread = jnp.concatenate(
        [
            jnp.sum(windows[k].astype(F32) * gram[:, k : k + 1], axis=0, keepdims=True)
            for k in range(blocks)
        ],
        axis=0,
    )
    current = compact[...]
    stepped = jnp.maximum(current + (product - spread) / norm, 0.0)
    stepped = jnp.where(current > 0, stepped, 0.0)
    height = 2 * SUBLANES
    for k in range(blocks):
        first, second, offset = split_run(starts[k], tiles)
        group = slice(k // height * height, k // height * height + height)
        chosen = row[group] == k
        for index, part in ((first, lane[group] >= offset), (second, lane[group] < offset)):
            at = lane_tile(index)
            old = out[group, at].astype(F32)
            out[group, at] = jnp.where(chosen & part, stepped[group], old).astype(out.dtype)


def finish(starts, shared, windows, compact, fresh, voxels):
    blocks = windows.shape[0]
    return pl.pallas_call(
        finish_kernel,
        in_specs=[SMEM, VMEM, VMEM, VMEM, VMEM],
        out_specs=[VMEM, VMEM],
        out_shape=[
            jax.ShapeDtypeStruct((blocks, voxels), BF16),
            jax.ShapeDtypeStruct(fresh.shape, fresh.dtype),
        ],
        compiler_params=PARAMS,
        name="finish",
    )(near_scalar(starts), near(shared), near(windows), near(compact), near(fresh))


def swapped(recording):
    count = lax.axis_size("bricks")
    across = [(i, i + 1) for i in range(1, count - 1, 2)]
    within = [(i, i + 1) for i in range(0, count, 2)]
    pair = lax.ppermute(recording, "bricks", within + [(b, a) for a, b in within])
    other = lax.ppermute(recording, "bricks", across + [(b, a) for a, b in across])
    return pair, other


def shards(recording, traces, footprints, block_owner, block_slot):
    voxels = footprints.shape[1]
    owners = lax.axis_size("bricks")
    groups = lax.axis_size("frames")
    pair, other = swapped(recording)
    owner = block_owner.T
    slot = block_slot[None, :]
    starts, windows, compact, corr, labels, piece = prepare(owner, slot, traces, footprints, owners)
    prior = lax.all_to_all(piece, "bricks", 0, 0)
    voxel_windows, projected = denoise_windows(starts, recording, pair, other, compact)
    partials, slot_prior = combine(prior, labels, projected, corr)
    gathered = lax.all_to_all(partials, "bricks", 0, 0)
    fresh, sent = update(
        prior, gathered, labels, traces, slot_prior, voxel_windows, groups
    )
    shared = lax.all_to_all(sent, "frames", 0, 0)
    footprints_new, traces_new = finish(starts, shared, windows, compact, fresh, voxels)
    return (traces_new, footprints_new)


def solution(mesh):
    return jax.shard_map(
        shards,
        mesh=mesh,
        in_specs=(
            P("frames", "bricks", None, None),
            P("frames", "bricks"),
            P("bricks", None),
            P("bricks", None),
            P("bricks"),
        ),
        out_specs=(P("frames", "bricks"), P("bricks", None)),
        check_vma=False,
    )
```

```python
import jax
import jax.numpy as jnp
from jax import lax
from jax.experimental import pallas as pl
from jax.experimental.pallas import tpu as pltpu
from jax.sharding import PartitionSpec as P


TIME_STEP = 0.14
HIGHEST = lax.Precision.HIGHEST
LANES = 128
SUBLANES = 8
F32 = jnp.float32
MARK_SCALE = 16384.0
BF16 = jnp.bfloat16
VMEM = pl.BlockSpec(memory_space=pltpu.VMEM)
SMEM = pl.BlockSpec(memory_space=pltpu.SMEM)
PARAMS = pltpu.CompilerParams(vmem_limit_bytes=16 * 2**20)


def near(array):
    return pltpu.with_memory_space_constraint(array, pltpu.VMEM)


def far(array):
    return pltpu.with_memory_space_constraint(array, pltpu.HBM)


def near_scalar(array):
    return pltpu.with_memory_space_constraint(array, pltpu.SMEM)


def iota(shape, axis):
    return lax.broadcasted_iota(jnp.int32, shape, axis)


def onehot(mask):
    return jnp.where(mask, 1.0, 0.0).astype(BF16)


def split_run(start, tiles):
    first = start >> 7
    return first, (first + 1) & (tiles - 1), start & (LANES - 1)


def lane_tile(index):
    return pl.ds(pl.multiple_of(index * LANES, LANES), LANES)


def two_terms(value):
    high = value.astype(BF16).astype(F32)
    return high, value - high


def as_column(line):
    count = line.shape[1]
    square = (count, count)
    same = iota(square, 0) == iota(square, 1)
    return jnp.sum(jnp.where(same, line, 0), axis=1, keepdims=True)


def label_rows(owner, slot, traces):
    frames, owned = traces.shape
    blocks = owner.shape[1]
    lane = iota((1, LANES), 1)
    gap = jnp.zeros((1, LANES - blocks), F32)
    lists = [jnp.concatenate([x[...].astype(F32), gap], axis=1) for x in (owner, slot)]
    rows = []
    for q in range(blocks // SUBLANES):
        first = pltpu.roll(lists[0], (LANES - q * SUBLANES) % LANES, 1)
        second = pltpu.roll(lists[1], (LANES + SUBLANES - q * SUBLANES) % LANES, 1)
        rows.append(
            jnp.where(lane < SUBLANES, first, jnp.where(lane < 2 * SUBLANES, second, 0.0))
        )
    wide = jnp.concatenate(
        [traces[...].astype(F32), jnp.zeros((frames, LANES - owned), F32)], axis=1
    )
    lane = iota((SUBLANES, LANES), 1)
    half = LANES // 2
    moved = jnp.where(
        lane < half + owned,
        pltpu.roll(wide[:SUBLANES], half, 1),
        pltpu.roll(wide[SUBLANES:], half + owned, 1),
    )
    return jnp.concatenate(rows + rows, axis=0) + jnp.where(lane < half, 0.0, moved)


def prepare_kernel(owner, slot, traces, foot, starts, windows, compact, corr, labels, piece):
    blocks, voxels = foot.shape
    tiles = voxels // LANES
    acc = jnp.zeros((blocks, LANES), BF16)
    for t in range(1, tiles):
        cell = foot[:, t * LANES : (t + 1) * LANES]
        acc = jnp.maximum(acc, jnp.minimum(cell, jnp.asarray(t / MARK_SCALE, BF16)))
    tile_of = acc.astype(F32) * MARK_SCALE
    lowest = jnp.min(tile_of, axis=1, keepdims=True)
    highest = jnp.max(tile_of, axis=1, keepdims=True)
    first_tile = jnp.where(highest - lowest > 1.5, highest, lowest)
    behind = jnp.sum(jnp.where(tile_of != first_tile, 1.0, 0.0), axis=1, keepdims=True)
    begin = (first_tile * LANES + behind).astype(jnp.int32)
    lane = iota((blocks, LANES), 1)
    row = iota((blocks, LANES), 0)
    sums = jnp.zeros((blocks, LANES), F32)
    for k in range(blocks):
        start = begin[k, 0]
        starts[k] = start
        first, second, offset = split_run(start, tiles)
        one = foot[:, lane_tile(first)].astype(F32)
        two = foot[:, lane_tile(second)].astype(F32)
        window = jnp.where(lane >= offset, one, two)
        windows[k] = window.astype(BF16)
        own = window[k : k + 1]
        compact[k : k + 1, :] = own
        sums = jnp.where(lane == k, jnp.sum(window * own, axis=1, keepdims=True), sums)
    corr[...] = sums
    labels[...] = jnp.where(lane == 0, as_column(owner[...]), as_column(slot[...]))
    diag = jnp.sum(jnp.where(lane == row, sums, 0.0), axis=1, keepdims=True)
    placed = jnp.where(lane == 2 * SUBLANES + row % SUBLANES, diag, 0.0)
    groups = blocks // SUBLANES
    rows = [
        jnp.sum(placed[q * SUBLANES : (q + 1) * SUBLANES], axis=0, keepdims=True)
        for q in range(groups)
    ]
    terms = [two_terms(r) for r in rows]
    part = jnp.concatenate([t[0] for t in terms] + [t[1] for t in terms], axis=0)
    whole = (label_rows(owner, slot, traces) + part).astype(BF16)
    piece[...] = jnp.broadcast_to(whole[None], piece.shape)


def prepare(owner, slot, traces, footprints, owners):
    blocks, _ = footprints.shape
    return pl.pallas_call(
        prepare_kernel,
        in_specs=[VMEM] * 4,
        out_specs=[SMEM, VMEM, VMEM, VMEM, VMEM, VMEM],
        out_shape=[
            pltpu.SMEM((blocks,), jnp.int32),
            pltpu.VMEM((blocks, blocks, LANES), BF16),
            pltpu.VMEM((blocks, LANES), F32),
            pltpu.VMEM((blocks, LANES), F32),
            pltpu.VMEM((blocks, LANES), jnp.int32),
            pltpu.VMEM((owners, SUBLANES, LANES), BF16),
        ],
        compiler_params=PARAMS,
        name="prepare",
    )(far(owner), far(slot), far(traces), far(footprints))


def flux_of(difference):
    return difference / (1.0 + difference * difference)


PITCH = 32
TOP = 8


def relax(planes, masks, held, passed, base):
    first_col, last_col = masks
    across = [
        [[flux_of(planes[i + 1][z][y] - planes[i][z][y]) for y in range(2)] for z in range(2)]
        for i in range(len(planes) - 1)
    ]
    out = []
    for i in range(1, len(planes) - 1):
        u = planes[i]
        edge = [[flux_of(u[0][0]), flux_of(u[0][1])], [flux_of(u[1][0]), None]]
        total = [[across[i][z][y] - across[i - 1][z][y] for y in range(2)] for z in range(2)]
        slot = (base + i - 1) * PITCH + TOP
        for y in range(2):
            for z in range(2):
                held[y, slot + z * SUBLANES : slot + (z + 1) * SUBLANES, :] = u[z][y]
            passed[y, slot - 1 : slot, :] = edge[0][y][:1]
            down = []
            for z in range(2):
                at = slot + z * SUBLANES
                down.append(flux_of(held[y, at + 1 : at + 1 + SUBLANES, :] - u[z][y]))
                passed[y, at : at + SUBLANES, :] = down[z]
            for z in range(2):
                at = slot + z * SUBLANES
                total[z][y] = total[z][y] + (down[z] - passed[y, at - 1 : at - 1 + SUBLANES, :])
        for z in range(2):
            low = pltpu.roll(u[z][0], LANES - 1, 1)
            high = pltpu.roll(u[z][1], LANES - 1, 1)
            right_low = flux_of(jnp.where(last_col, high, low) - u[z][0])
            right_high = flux_of(jnp.where(last_col, 0.0, high) - u[z][1])
            left_low = pltpu.roll(right_low, 1, 1)
            left_high = pltpu.roll(right_high, 1, 1)
            total[z][0] = total[z][0] + (right_low - jnp.where(first_col, edge[z][0], left_low))
            total[z][1] = total[z][1] + (right_high - jnp.where(first_col, left_low, left_high))
        out.append([[u[z][y] + TIME_STEP * total[z][y] for y in range(2)] for z in range(2)])
    return out


def quarters(plane):
    wide = plane.astype(F32)
    return [
        [wide[z * SUBLANES : (z + 1) * SUBLANES, y * LANES : (y + 1) * LANES] for y in range(2)]
        for z in range(2)
    ]


def scaled(plane, keep):
    return [[cell * keep for cell in line] for line in plane]


def denoise_kernel(
    starts, rec, pair, other, compact, voxel_windows, projected, field, held, passed
):
    frames, planes, rows, _ = rec.shape
    width = 3
    position = lax.axis_index("bricks")
    low_keep = jnp.where(position > 0, 1.0, 0.0)
    high_keep = jnp.where(position < lax.axis_size("bricks") - 1, 1.0, 0.0)
    col = iota((SUBLANES, LANES), 1)
    masks = (col == 0, col == LANES - 1)
    held[...] = jnp.zeros(held.shape, F32)

    def one_frame(f, low, high, lane_of):
        u = [quarters(low[f, planes - width + i]) for i in range(width)]
        u = u + [quarters(rec[f, i]) for i in range(planes)]
        u = u + [quarters(high[f, i]) for i in range(width)]
        base = lane_of * width * (planes + 2)
        for sweep in range(width):
            u = relax(u, masks, held, passed, base)
            base += len(u)
            extra = width - 1 - sweep
            if extra:
                u = (
                    [scaled(v, low_keep) for v in u[:extra]]
                    + u[extra : extra + planes]
                    + [scaled(v, high_keep) for v in u[extra + planes :]]
                )
        for i in range(planes):
            for z in range(2):
                for y in range(2):
                    at = pl.ds((i * rows + z * SUBLANES) * frames + f, SUBLANES, stride=frames)
                    field[y, at, :] = u[i][z][y].astype(BF16).astype(F32)

    odd = position % 2 == 1
    for is_odd, low, high in ((True, pair, other), (False, other, pair)):

        @pl.when(odd if is_odd else jnp.logical_not(odd))
        def _(low=low, high=high):
            @pl.loop(0, frames // 2)
            def _(g):
                one_frame(2 * g, low, high, 0)
                one_frame(2 * g + 1, low, high, 1)

    blocks = compact.shape[0]
    tiles = planes * rows * 2
    lane = iota((frames, LANES), 1)
    acc = jnp.zeros((frames, LANES), F32)
    for k in range(blocks):
        first, second, offset = split_run(starts[k], tiles)
        one = field[first & 1, pl.ds(pl.multiple_of((first >> 1) * frames, frames), frames), :]
        two = field[second & 1, pl.ds(pl.multiple_of((second >> 1) * frames, frames), frames), :]
        window = jnp.where(lane >= offset, one, two)
        voxel_windows[k] = window
        column = jnp.sum(window * compact[k : k + 1, :], axis=1, keepdims=True)
        acc = jnp.where(lane == k, column, acc)
    projected[...] = acc


def denoise_windows(starts, recording, pair, other, compact):
    frames, planes, rows, _ = recording.shape
    blocks = compact.shape[0]
    return pl.pallas_call(
        denoise_kernel,
        in_specs=[SMEM, VMEM, VMEM, VMEM, VMEM],
        out_specs=[VMEM, VMEM],
        out_shape=[
            pltpu.VMEM((blocks, frames, LANES), F32),
            pltpu.VMEM((frames, LANES), F32),
        ],
        scratch_shapes=[
            pltpu.VMEM((2, frames * planes * rows, LANES), F32),
            pltpu.VMEM((2, 6 * (planes + 2) * PITCH, LANES), F32),
            pltpu.VMEM((2, 6 * (planes + 2) * PITCH, LANES), F32),
        ],
        compiler_params=PARAMS,
        name="denoise",
    )(near_scalar(starts), near(recording), near(pair), near(other), near(compact))


def combine_kernel(prior, labels, projected, corr, piece, slot_prior):
    owners = prior.shape[0]
    blocks = corr.shape[0]
    frames = projected.shape[0]
    span = owners * SUBLANES
    flat = prior[...].astype(F32).reshape(span, LANES).astype(BF16)
    owner = labels[:, 0:1]
    slot = labels[:, 1:2]
    source = iota((blocks, span), 1)
    pick = jnp.concatenate(
        [onehot(source == owner * SUBLANES + i) for i in range(SUBLANES)], axis=0
    )
    found = jnp.dot(pick, flat, preferred_element_type=F32)
    lane = iota((blocks, LANES), 1)
    wanted = (lane >= LANES // 2) & (lane % blocks == slot)
    parts = [
        jnp.where(wanted, found[i * blocks : (i + 1) * blocks], 0.0).astype(BF16)
        for i in range(SUBLANES)
    ]
    wide = SUBLANES * LANES
    here = iota((wide, LANES), 0)
    frame_of = here // LANES + (here % LANES - LANES // 2) // blocks * SUBLANES
    frame_of = jnp.where(here % LANES >= LANES // 2, frame_of, -1)
    spread = onehot(frame_of == iota((wide, LANES), 1) % frames)
    earlier = jnp.dot(jnp.concatenate(parts, axis=1), spread, preferred_element_type=F32)
    slot_prior[...] = earlier
    repeat = jnp.where(
        iota((frames, LANES), 0) == iota((frames, LANES), 1) % frames, 1.0, 0.0
    )
    tiled = lax.dot_general(
        projected[...],
        repeat,
        (((0,), (0,)), ((), ())),
        precision=HIGHEST,
        preferred_element_type=F32,
    )[:blocks]
    value = tiled - jnp.dot(
        corr[:, :blocks], earlier, precision=HIGHEST, preferred_element_type=F32
    )
    row = iota((blocks, LANES), 0)
    value = jnp.where(lane // frames == row % SUBLANES, value, 0.0)
    lines = [
        jnp.sum(value[q * SUBLANES : (q + 1) * SUBLANES], axis=0, keepdims=True)
        for q in range(blocks // SUBLANES)
    ]
    terms = [two_terms(v) for v in lines]
    whole = jnp.concatenate([t[0] for t in terms] + [t[1] for t in terms], axis=0).astype(BF16)
    piece[...] = jnp.broadcast_to(whole[None], piece.shape)


def combine(prior, labels, projected, corr):
    blocks = corr.shape[0]
    return pl.pallas_call(
        combine_kernel,
        in_specs=[VMEM] * 4,
        out_specs=[VMEM, VMEM],
        out_shape=[
            pltpu.VMEM(prior.shape, BF16),
            pltpu.VMEM((blocks, LANES), F32),
        ],
        compiler_params=PARAMS,
        name="combine",
    )(near(prior), near(labels), near(projected), near(corr))


def update_kernel(
    prior, gathered, labels, traces, slot_prior, voxel_windows, traces_new, sent
):
    owners = prior.shape[0]
    blocks = slot_prior.shape[0]
    frames, owned = traces.shape
    span = owners * SUBLANES
    flat = prior[...].astype(F32).reshape(span, LANES).astype(BF16)
    values = gathered[...].astype(F32).reshape(span, LANES).astype(BF16)
    lead = 4 * SUBLANES
    picks = onehot(iota((lead, LANES), 0) == iota((lead, LANES), 1))
    lists = lax.dot_general(
        picks, flat, (((1,), (1,)), ((), ())), preferred_element_type=F32
    )
    comps = lists[:SUBLANES] * float(owned) + lists[SUBLANES : 2 * SUBLANES]
    diags = lists[2 * SUBLANES : 3 * SUBLANES]
    position = lax.axis_index("bricks")
    asked = labels[:, 0:1] * owned + labels[:, 1:2]
    held = position * owned + iota((owned, 1), 0)
    target = jnp.concatenate([asked, held], axis=0).astype(F32)
    count = blocks + owned
    matches = []
    weight = jnp.zeros((count, span), F32)
    for j in range(SUBLANES):
        match = comps[j : j + 1] == target
        matches.append(onehot(match))
        weight = weight + jnp.where(match, diags[j : j + 1], 0.0)
    weight = jnp.sum(weight, axis=1, keepdims=True)
    sums = jnp.dot(jnp.concatenate(matches, axis=0), values, preferred_element_type=F32)
    group = iota((count, LANES), 1) // frames
    total = jnp.zeros((count, LANES), F32)
    for j in range(SUBLANES):
        total = jnp.where(group == j, sums[j * count : (j + 1) * count], total)
    shift = LANES // 2
    while shift >= frames:
        total = total + pltpu.roll(total, shift, 1)
        shift //= 2
    repeat = onehot(iota((frames, LANES), 0) == iota((frames, LANES), 1) % frames)
    mine = lax.dot_general(
        traces[...], repeat, (((0,), (0,)), ((), ())), preferred_element_type=F32
    )
    before = jnp.concatenate([slot_prior[...], mine], axis=0)
    after = jnp.maximum(0.0, before + total / (weight + 1.0))
    padded = jnp.concatenate([after, jnp.zeros((LANES - count, LANES), F32)], axis=0)
    turned = padded.T
    traces_new[...] = turned[:frames, blocks:count]
    slots = turned[:frames].astype(BF16).astype(F32)
    lane = iota((SUBLANES, LANES), 1)
    packed = jnp.where(
        lane < blocks,
        slots[:SUBLANES],
        jnp.where(lane < 2 * blocks, pltpu.roll(slots[SUBLANES:], blocks, 1), 0.0),
    )
    for k in range(blocks):
        line = jnp.sum(voxel_windows[k] * slots[:, k : k + 1], axis=0, keepdims=True)
        for g in range(sent.shape[0]):
            sent[g, k : k + 1, :] = line
    for g in range(sent.shape[0]):
        sent[g, blocks : blocks + SUBLANES, :] = packed


def update(prior, gathered, labels, traces, slot_prior, voxel_windows, groups):
    blocks = slot_prior.shape[0]
    return pl.pallas_call(
        update_kernel,
        in_specs=[VMEM] * 6,
        out_specs=[VMEM, VMEM],
        out_shape=[
            pltpu.VMEM(traces.shape, F32),
            pltpu.VMEM((groups, blocks + SUBLANES, LANES), F32),
        ],
        compiler_params=PARAMS,
        name="update",
    )(
        near(prior),
        near(gathered),
        near(labels),
        near(traces),
        near(slot_prior),
        near(voxel_windows),
    )


def finish_kernel(starts, shared, windows, compact, fresh, out, traces_new):
    traces_new[...] = fresh[...]
    blocks, voxels = out.shape
    tiles = voxels // LANES
    groups = shared.shape[0]
    lane = iota((blocks, LANES), 1)
    row = iota((blocks, LANES), 0)
    out[...] = jnp.zeros(out.shape, out.dtype)
    product = shared[0, :blocks, :]
    for g in range(1, groups):
        product = product + shared[g, :blocks, :]
    slots = jnp.concatenate([shared[g, blocks:, :] for g in range(groups)], axis=0).astype(BF16)
    both = lax.dot_general(slots, slots, (((0,), (0,)), ((), ())), preferred_element_type=F32)
    gram = both[:blocks] + pltpu.roll(both[blocks : 2 * blocks], LANES - blocks, 1)
    norm = jnp.sum(jnp.where(lane == row, gram, 0.0), axis=1, keepdims=True) + 1.0
    spread = jnp.concatenate(
        [
            jnp.sum(windows[k].astype(F32) * gram[:, k : k + 1], axis=0, keepdims=True)
            for k in range(blocks)
        ],
        axis=0,
    )
    current = compact[...]
    stepped = jnp.maximum(current + (product - spread) / norm, 0.0)
    stepped = jnp.where(current > 0, stepped, 0.0)
    height = 2 * SUBLANES
    for k in range(blocks):
        first, second, offset = split_run(starts[k], tiles)
        group = slice(k // height * height, k // height * height + height)
        chosen = row[group] == k
        for index, part in ((first, lane[group] >= offset), (second, lane[group] < offset)):
            at = lane_tile(index)
            old = out[group, at].astype(F32)
            out[group, at] = jnp.where(chosen & part, stepped[group], old).astype(out.dtype)


def finish(starts, shared, windows, compact, fresh, voxels):
    blocks = windows.shape[0]
    return pl.pallas_call(
        finish_kernel,
        in_specs=[SMEM, VMEM, VMEM, VMEM, VMEM],
        out_specs=[VMEM, VMEM],
        out_shape=[
            jax.ShapeDtypeStruct((blocks, voxels), BF16),
            jax.ShapeDtypeStruct(fresh.shape, fresh.dtype),
        ],
        compiler_params=PARAMS,
        name="finish",
    )(near_scalar(starts), near(shared), near(windows), near(compact), near(fresh))


def swapped(recording):
    count = lax.axis_size("bricks")
    across = [(i, i + 1) for i in range(1, count - 1, 2)]
    within = [(i, i + 1) for i in range(0, count, 2)]
    pair = lax.ppermute(recording, "bricks", within + [(b, a) for a, b in within])
    other = lax.ppermute(recording, "bricks", across + [(b, a) for a, b in across])
    return pair, other


def shards(recording, traces, footprints, block_owner, block_slot):
    voxels = footprints.shape[1]
    owners = lax.axis_size("bricks")
    groups = lax.axis_size("frames")
    pair, other = swapped(recording)
    owner = block_owner.T
    slot = block_slot[None, :]
    starts, windows, compact, corr, labels, piece = prepare(owner, slot, traces, footprints, owners)
    prior = lax.all_to_all(piece, "bricks", 0, 0)
    voxel_windows, projected = denoise_windows(starts, recording, pair, other, compact)
    partials, slot_prior = combine(prior, labels, projected, corr)
    gathered = lax.all_to_all(partials, "bricks", 0, 0)
    fresh, sent = update(
        prior, gathered, labels, traces, slot_prior, voxel_windows, groups
    )
    shared = lax.all_to_all(sent, "frames", 0, 0)
    footprints_new, traces_new = finish(starts, shared, windows, compact, fresh, voxels)
    return (traces_new, footprints_new)


def solution(mesh):
    return jax.shard_map(
        shards,
        mesh=mesh,
        in_specs=(
            P("frames", "bricks", None, None),
            P("frames", "bricks"),
            P("bricks", None),
            P("bricks", None),
            P("bricks"),
        ),
        out_specs=(P("frames", "bricks"), P("bricks", None)),
        check_vma=False,
    )
```

```python
import jax
import jax.numpy as jnp
from jax import lax
from jax.experimental import pallas as pl
from jax.experimental.pallas import tpu as pltpu
from jax.sharding import PartitionSpec as P


TIME_STEP = 0.14
HIGHEST = lax.Precision.HIGHEST
LANES = 128
SUBLANES = 8
F32 = jnp.float32
MARK_SCALE = 16384.0
BF16 = jnp.bfloat16
VMEM = pl.BlockSpec(memory_space=pltpu.VMEM)
SMEM = pl.BlockSpec(memory_space=pltpu.SMEM)
PARAMS = pltpu.CompilerParams(vmem_limit_bytes=16 * 2**20)


def near(array):
    return pltpu.with_memory_space_constraint(array, pltpu.VMEM)


def far(array):
    return pltpu.with_memory_space_constraint(array, pltpu.HBM)


def near_scalar(array):
    return pltpu.with_memory_space_constraint(array, pltpu.SMEM)


def iota(shape, axis):
    return lax.broadcasted_iota(jnp.int32, shape, axis)


def onehot(mask):
    return jnp.where(mask, 1.0, 0.0).astype(BF16)


def split_run(start, tiles):
    first = start >> 7
    return first, (first + 1) & (tiles - 1), start & (LANES - 1)


def lane_tile(index):
    return pl.ds(pl.multiple_of(index * LANES, LANES), LANES)


def two_terms(value):
    high = value.astype(BF16).astype(F32)
    return high, value - high


def as_column(line):
    count = line.shape[1]
    square = (count, count)
    same = iota(square, 0) == iota(square, 1)
    return jnp.sum(jnp.where(same, line, 0), axis=1, keepdims=True)


def label_rows(owner, slot, traces):
    frames, owned = traces.shape
    blocks = owner.shape[1]
    lane = iota((1, LANES), 1)
    gap = jnp.zeros((1, LANES - blocks), F32)
    lists = [jnp.concatenate([x[...].astype(F32), gap], axis=1) for x in (owner, slot)]
    rows = []
    for q in range(blocks // SUBLANES):
        first = pltpu.roll(lists[0], (LANES - q * SUBLANES) % LANES, 1)
        second = pltpu.roll(lists[1], (LANES + SUBLANES - q * SUBLANES) % LANES, 1)
        rows.append(
            jnp.where(lane < SUBLANES, first, jnp.where(lane < 2 * SUBLANES, second, 0.0))
        )
    wide = jnp.concatenate(
        [traces[...].astype(F32), jnp.zeros((frames, LANES - owned), F32)], axis=1
    )
    lane = iota((SUBLANES, LANES), 1)
    half = LANES // 2
    moved = jnp.where(
        lane < half + owned,
        pltpu.roll(wide[:SUBLANES], half, 1),
        pltpu.roll(wide[SUBLANES:], half + owned, 1),
    )
    return jnp.concatenate(rows + rows, axis=0) + jnp.where(lane < half, 0.0, moved)


def prepare_kernel(
    owner, slot, traces, foot, starts, windows, compact, corr, labels, places, piece
):
    blocks, voxels = foot.shape
    tiles = voxels // LANES
    acc = jnp.zeros((blocks, LANES), BF16)
    for t in range(1, tiles):
        cell = foot[:, t * LANES : (t + 1) * LANES]
        acc = jnp.maximum(acc, jnp.minimum(cell, jnp.asarray(t / MARK_SCALE, BF16)))
    places[...] = acc
    tile_of = acc.astype(F32) * MARK_SCALE
    lowest = jnp.min(tile_of, axis=1, keepdims=True)
    highest = jnp.max(tile_of, axis=1, keepdims=True)
    first_tile = jnp.where(highest - lowest > 1.5, highest, lowest)
    behind = jnp.sum(jnp.where(tile_of != first_tile, 1.0, 0.0), axis=1, keepdims=True)
    begin = (first_tile * LANES + behind).astype(jnp.int32)
    lane = iota((blocks, LANES), 1)
    row = iota((blocks, LANES), 0)
    sums = jnp.zeros((blocks, LANES), F32)
    for k in range(blocks):
        start = begin[k, 0]
        starts[k] = start
        first, second, offset = split_run(start, tiles)
        one = foot[:, lane_tile(first)].astype(F32)
        two = foot[:, lane_tile(second)].astype(F32)
        window = jnp.where(lane >= offset, one, two)
        windows[k] = window.astype(BF16)
        own = window[k : k + 1]
        compact[k : k + 1, :] = own
        sums = jnp.where(lane == k, jnp.sum(window * own, axis=1, keepdims=True), sums)
    corr[...] = sums
    labels[...] = jnp.where(lane == 0, as_column(owner[...]), as_column(slot[...]))
    diag = jnp.sum(jnp.where(lane == row, sums, 0.0), axis=1, keepdims=True)
    placed = jnp.where(lane == 2 * SUBLANES + row % SUBLANES, diag, 0.0)
    groups = blocks // SUBLANES
    rows = [
        jnp.sum(placed[q * SUBLANES : (q + 1) * SUBLANES], axis=0, keepdims=True)
        for q in range(groups)
    ]
    terms = [two_terms(r) for r in rows]
    part = jnp.concatenate([t[0] for t in terms] + [t[1] for t in terms], axis=0)
    whole = (label_rows(owner, slot, traces) + part).astype(BF16)
    piece[...] = jnp.broadcast_to(whole[None], piece.shape)


def prepare(owner, slot, traces, footprints, owners):
    blocks, _ = footprints.shape
    return pl.pallas_call(
        prepare_kernel,
        in_specs=[VMEM] * 4,
        out_specs=[SMEM] + [VMEM] * 6,
        out_shape=[
            pltpu.SMEM((blocks,), jnp.int32),
            pltpu.VMEM((blocks, blocks, LANES), BF16),
            pltpu.VMEM((blocks, LANES), F32),
            pltpu.VMEM((blocks, LANES), F32),
            pltpu.VMEM((blocks, LANES), jnp.int32),
            pltpu.VMEM((blocks, LANES), BF16),
            pltpu.VMEM((owners, SUBLANES, LANES), BF16),
        ],
        compiler_params=PARAMS,
        name="prepare",
    )(far(owner), far(slot), far(traces), far(footprints))


def flux_of(difference):
    return difference / (1.0 + difference * difference)


PITCH = 32
TOP = 8
AT_ONCE = 2


def relax(planes, masks, held, passed, base):
    first_col, last_col = masks
    across = [
        [[flux_of(planes[i + 1][z][y] - planes[i][z][y]) for y in range(2)] for z in range(2)]
        for i in range(len(planes) - 1)
    ]
    out = []
    for i in range(1, len(planes) - 1):
        u = planes[i]
        edge = [[flux_of(u[0][0]), flux_of(u[0][1])], [flux_of(u[1][0]), None]]
        total = [[across[i][z][y] - across[i - 1][z][y] for y in range(2)] for z in range(2)]
        slot = (base + i - 1) * PITCH + TOP
        for y in range(2):
            for z in range(2):
                held[y, slot + z * SUBLANES : slot + (z + 1) * SUBLANES, :] = u[z][y]
            passed[y, slot - 1 : slot, :] = edge[0][y][:1]
            down = []
            for z in range(2):
                at = slot + z * SUBLANES
                down.append(flux_of(held[y, at + 1 : at + 1 + SUBLANES, :] - u[z][y]))
                passed[y, at : at + SUBLANES, :] = down[z]
            for z in range(2):
                at = slot + z * SUBLANES
                total[z][y] = total[z][y] + (down[z] - passed[y, at - 1 : at - 1 + SUBLANES, :])
        for z in range(2):
            low = pltpu.roll(u[z][0], LANES - 1, 1)
            high = pltpu.roll(u[z][1], LANES - 1, 1)
            right_low = flux_of(jnp.where(last_col, high, low) - u[z][0])
            right_high = flux_of(jnp.where(last_col, 0.0, high) - u[z][1])
            left_low = pltpu.roll(right_low, 1, 1)
            left_high = pltpu.roll(right_high, 1, 1)
            total[z][0] = total[z][0] + (right_low - jnp.where(first_col, edge[z][0], left_low))
            total[z][1] = total[z][1] + (right_high - jnp.where(first_col, left_low, left_high))
        out.append([[u[z][y] + TIME_STEP * total[z][y] for y in range(2)] for z in range(2)])
    return out


def quarters(plane):
    wide = plane.astype(F32)
    return [
        [wide[z * SUBLANES : (z + 1) * SUBLANES, y * LANES : (y + 1) * LANES] for y in range(2)]
        for z in range(2)
    ]


def scaled(plane, keep):
    return [[cell * keep for cell in line] for line in plane]


def denoise_kernel(
    starts, rec, pair, other, compact, voxel_windows, projected, field, held, passed
):
    frames, planes, rows, _ = rec.shape
    width = 3
    position = lax.axis_index("bricks")
    low_keep = jnp.where(position > 0, 1.0, 0.0)
    high_keep = jnp.where(position < lax.axis_size("bricks") - 1, 1.0, 0.0)
    col = iota((SUBLANES, LANES), 1)
    masks = (col == 0, col == LANES - 1)
    held[...] = jnp.zeros(held.shape, F32)

    def one_frame(f, low, high, lane_of):
        u = [quarters(low[f, planes - width + i]) for i in range(width)]
        u = u + [quarters(rec[f, i]) for i in range(planes)]
        u = u + [quarters(high[f, i]) for i in range(width)]
        base = lane_of * width * (planes + 2)
        for sweep in range(width):
            u = relax(u, masks, held, passed, base)
            base += len(u)
            extra = width - 1 - sweep
            if extra:
                u = (
                    [scaled(v, low_keep) for v in u[:extra]]
                    + u[extra : extra + planes]
                    + [scaled(v, high_keep) for v in u[extra + planes :]]
                )
        for i in range(planes):
            for z in range(2):
                for y in range(2):
                    at = pl.ds((i * rows + z * SUBLANES) * frames + f, SUBLANES, stride=frames)
                    field[y, at, :] = u[i][z][y].astype(BF16).astype(F32)

    odd = position % 2 == 1
    for is_odd, low, high in ((True, pair, other), (False, other, pair)):

        @pl.when(odd if is_odd else jnp.logical_not(odd))
        def _(low=low, high=high):
            @pl.loop(0, frames // AT_ONCE)
            def _(g):
                for part in range(AT_ONCE):
                    one_frame(AT_ONCE * g + part, low, high, part)

    blocks = compact.shape[0]
    tiles = planes * rows * 2
    lane = iota((frames, LANES), 1)
    acc = jnp.zeros((frames, LANES), F32)
    for k in range(blocks):
        first, second, offset = split_run(starts[k], tiles)
        one = field[first & 1, pl.ds(pl.multiple_of((first >> 1) * frames, frames), frames), :]
        two = field[second & 1, pl.ds(pl.multiple_of((second >> 1) * frames, frames), frames), :]
        window = jnp.where(lane >= offset, one, two)
        voxel_windows[k] = window
        column = jnp.sum(window * compact[k : k + 1, :], axis=1, keepdims=True)
        acc = jnp.where(lane == k, column, acc)
    projected[...] = acc


def denoise_windows(starts, recording, pair, other, compact):
    frames, planes, rows, _ = recording.shape
    blocks = compact.shape[0]
    return pl.pallas_call(
        denoise_kernel,
        in_specs=[SMEM, VMEM, VMEM, VMEM, VMEM],
        out_specs=[VMEM, VMEM],
        out_shape=[
            pltpu.VMEM((blocks, frames, LANES), F32),
            pltpu.VMEM((frames, LANES), F32),
        ],
        scratch_shapes=[
            pltpu.VMEM((2, frames * planes * rows, LANES), F32),
            pltpu.VMEM((2, 3 * AT_ONCE * (planes + 2) * PITCH, LANES), F32),
            pltpu.VMEM((2, 3 * AT_ONCE * (planes + 2) * PITCH, LANES), F32),
        ],
        compiler_params=PARAMS,
        name="denoise",
    )(near_scalar(starts), near(recording), near(pair), near(other), near(compact))


def combine_kernel(prior, labels, projected, corr, piece, slot_prior):
    owners = prior.shape[0]
    blocks = corr.shape[0]
    frames = projected.shape[0]
    span = owners * SUBLANES
    flat = prior[...].astype(F32).reshape(span, LANES).astype(BF16)
    owner = labels[:, 0:1]
    slot = labels[:, 1:2]
    source = iota((blocks, span), 1)
    pick = jnp.concatenate(
        [onehot(source == owner * SUBLANES + i) for i in range(SUBLANES)], axis=0
    )
    found = jnp.dot(pick, flat, preferred_element_type=F32)
    lane = iota((blocks, LANES), 1)
    wanted = (lane >= LANES // 2) & (lane % blocks == slot)
    parts = [
        jnp.where(wanted, found[i * blocks : (i + 1) * blocks], 0.0).astype(BF16)
        for i in range(SUBLANES)
    ]
    wide = SUBLANES * LANES
    here = iota((wide, LANES), 0)
    frame_of = here // LANES + (here % LANES - LANES // 2) // blocks * SUBLANES
    frame_of = jnp.where(here % LANES >= LANES // 2, frame_of, -1)
    spread = onehot(frame_of == iota((wide, LANES), 1) % frames)
    earlier = jnp.dot(jnp.concatenate(parts, axis=1), spread, preferred_element_type=F32)
    slot_prior[...] = earlier
    repeat = jnp.where(
        iota((frames, LANES), 0) == iota((frames, LANES), 1) % frames, 1.0, 0.0
    )
    tiled = lax.dot_general(
        projected[...],
        repeat,
        (((0,), (0,)), ((), ())),
        precision=HIGHEST,
        preferred_element_type=F32,
    )[:blocks]
    value = tiled - jnp.dot(
        corr[:, :blocks], earlier, precision=HIGHEST, preferred_element_type=F32
    )
    row = iota((blocks, LANES), 0)
    value = jnp.where(lane // frames == row % SUBLANES, value, 0.0)
    lines = [
        jnp.sum(value[q * SUBLANES : (q + 1) * SUBLANES], axis=0, keepdims=True)
        for q in range(blocks // SUBLANES)
    ]
    terms = [two_terms(v) for v in lines]
    whole = jnp.concatenate([t[0] for t in terms] + [t[1] for t in terms], axis=0).astype(BF16)
    piece[...] = jnp.broadcast_to(whole[None], piece.shape)


def combine(prior, labels, projected, corr):
    blocks = corr.shape[0]
    return pl.pallas_call(
        combine_kernel,
        in_specs=[VMEM] * 4,
        out_specs=[VMEM, VMEM],
        out_shape=[
            pltpu.VMEM(prior.shape, BF16),
            pltpu.VMEM((blocks, LANES), F32),
        ],
        compiler_params=PARAMS,
        name="combine",
    )(near(prior), near(labels), near(projected), near(corr))


def update_kernel(
    prior, gathered, labels, traces, slot_prior, voxel_windows, traces_new, sent
):
    owners = prior.shape[0]
    blocks = slot_prior.shape[0]
    frames, owned = traces.shape
    span = owners * SUBLANES
    flat = prior[...].astype(F32).reshape(span, LANES).astype(BF16)
    values = gathered[...].astype(F32).reshape(span, LANES).astype(BF16)
    lead = 4 * SUBLANES
    picks = onehot(iota((lead, LANES), 0) == iota((lead, LANES), 1))
    lists = lax.dot_general(
        picks, flat, (((1,), (1,)), ((), ())), preferred_element_type=F32
    )
    comps = lists[:SUBLANES] * float(owned) + lists[SUBLANES : 2 * SUBLANES]
    diags = lists[2 * SUBLANES : 3 * SUBLANES]
    position = lax.axis_index("bricks")
    asked = labels[:, 0:1] * owned + labels[:, 1:2]
    held = position * owned + iota((owned, 1), 0)
    target = jnp.concatenate([asked, held], axis=0).astype(F32)
    count = blocks + owned
    matches = []
    weight = jnp.zeros((count, span), F32)
    for j in range(SUBLANES):
        match = comps[j : j + 1] == target
        matches.append(onehot(match))
        weight = weight + jnp.where(match, diags[j : j + 1], 0.0)
    weight = jnp.sum(weight, axis=1, keepdims=True)
    sums = jnp.dot(jnp.concatenate(matches, axis=0), values, preferred_element_type=F32)
    group = iota((count, LANES), 1) // frames
    total = jnp.zeros((count, LANES), F32)
    for j in range(SUBLANES):
        total = jnp.where(group == j, sums[j * count : (j + 1) * count], total)
    shift = LANES // 2
    while shift >= frames:
        total = total + pltpu.roll(total, shift, 1)
        shift //= 2
    repeat = onehot(iota((frames, LANES), 0) == iota((frames, LANES), 1) % frames)
    mine = lax.dot_general(
        traces[...], repeat, (((0,), (0,)), ((), ())), preferred_element_type=F32
    )
    before = jnp.concatenate([slot_prior[...], mine], axis=0)
    after = jnp.maximum(0.0, before + total / (weight + 1.0))
    padded = jnp.concatenate([after, jnp.zeros((LANES - count, LANES), F32)], axis=0)
    turned = padded.T
    traces_new[...] = turned[:frames, blocks:count]
    slots = turned[:frames].astype(BF16).astype(F32)
    lane = iota((SUBLANES, LANES), 1)
    packed = jnp.where(
        lane < blocks,
        slots[:SUBLANES],
        jnp.where(lane < 2 * blocks, pltpu.roll(slots[SUBLANES:], blocks, 1), 0.0),
    )
    for k in range(blocks):
        line = jnp.sum(voxel_windows[k] * slots[:, k : k + 1], axis=0, keepdims=True)
        sent[0, k : k + 1, :] = line
    sent[0, blocks : blocks + SUBLANES, :] = packed
    whole = sent[0]
    for g in range(1, sent.shape[0]):
        sent[g] = whole


def update(prior, gathered, labels, traces, slot_prior, voxel_windows, groups):
    blocks = slot_prior.shape[0]
    return pl.pallas_call(
        update_kernel,
        in_specs=[VMEM] * 6,
        out_specs=[VMEM, VMEM],
        out_shape=[
            pltpu.VMEM(traces.shape, F32),
            pltpu.VMEM((groups, blocks + SUBLANES, LANES), F32),
        ],
        compiler_params=PARAMS,
        name="update",
    )(
        near(prior),
        near(gathered),
        near(labels),
        near(traces),
        near(slot_prior),
        near(voxel_windows),
    )


def finish_kernel(places, shared, windows, compact, fresh, out, traces_new):
    traces_new[...] = fresh[...]
    blocks, voxels = out.shape
    tiles = voxels // LANES
    groups = shared.shape[0]
    lane = iota((blocks, LANES), 1)
    row = iota((blocks, LANES), 0)
    product = shared[0, :blocks, :]
    for g in range(1, groups):
        product = product + shared[g, :blocks, :]
    slots = jnp.concatenate([shared[g, blocks:, :] for g in range(groups)], axis=0).astype(BF16)
    both = lax.dot_general(slots, slots, (((0,), (0,)), ((), ())), preferred_element_type=F32)
    gram = both[:blocks] + pltpu.roll(both[blocks : 2 * blocks], LANES - blocks, 1)
    norm = jnp.sum(jnp.where(lane == row, gram, 0.0), axis=1, keepdims=True) + 1.0
    spread = jnp.concatenate(
        [
            jnp.sum(windows[k].astype(F32) * gram[:, k : k + 1], axis=0, keepdims=True)
            for k in range(blocks)
        ],
        axis=0,
    )
    current = compact[...]
    stepped = jnp.maximum(current + (product - spread) / norm, 0.0)
    stepped = jnp.where(current > 0, stepped, 0.0)
    final = stepped.astype(out.dtype)
    nothing = jnp.zeros(final.shape, out.dtype)
    place = places[...]
    for t in range(tiles):
        here = place == jnp.asarray(t / MARK_SCALE, BF16)
        out[:, t * LANES : (t + 1) * LANES] = jnp.where(here, final, nothing)


def finish(places, shared, windows, compact, fresh, voxels):
    blocks = windows.shape[0]
    return pl.pallas_call(
        finish_kernel,
        in_specs=[VMEM] * 5,
        out_specs=[VMEM, VMEM],
        out_shape=[
            jax.ShapeDtypeStruct((blocks, voxels), BF16),
            jax.ShapeDtypeStruct(fresh.shape, fresh.dtype),
        ],
        compiler_params=PARAMS,
        name="finish",
    )(near(places), near(shared), near(windows), near(compact), near(fresh))


def swapped(recording):
    count = lax.axis_size("bricks")
    across = [(i, i + 1) for i in range(1, count - 1, 2)]
    within = [(i, i + 1) for i in range(0, count, 2)]
    pair = lax.ppermute(recording, "bricks", within + [(b, a) for a, b in within])
    other = lax.ppermute(recording, "bricks", across + [(b, a) for a, b in across])
    return pair, other


def shards(recording, traces, footprints, block_owner, block_slot):
    voxels = footprints.shape[1]
    owners = lax.axis_size("bricks")
    groups = lax.axis_size("frames")
    pair, other = swapped(recording)
    owner = block_owner.T
    slot = block_slot[None, :]
    starts, windows, compact, corr, labels, places, piece = prepare(
        owner, slot, traces, footprints, owners
    )
    prior = lax.all_to_all(piece, "bricks", 0, 0)
    voxel_windows, projected = denoise_windows(starts, recording, pair, other, compact)
    partials, slot_prior = combine(prior, labels, projected, corr)
    gathered = lax.all_to_all(partials, "bricks", 0, 0)
    fresh, sent = update(
        prior, gathered, labels, traces, slot_prior, voxel_windows, groups
    )
    shared = lax.all_to_all(sent, "frames", 0, 0)
    footprints_new, traces_new = finish(places, shared, windows, compact, fresh, voxels)
    return (traces_new, footprints_new)


def solution(mesh):
    return jax.shard_map(
        shards,
        mesh=mesh,
        in_specs=(
            P("frames", "bricks", None, None),
            P("frames", "bricks"),
            P("bricks", None),
            P("bricks", None),
            P("bricks"),
        ),
        out_specs=(P("frames", "bricks"), P("bricks", None)),
        check_vma=False,
    )
```
